256 devices in a mesh: cluster: 16 (over y_hi, z), client: 16 (over x, y_lo, core).
Axes of the slice: x: 4, y: 4 (y_hi: 2, y_lo: 2; y = y_hi * 2 + y_lo), z: 8, core: 2. Of those that a mesh axis runs over, the one named last changes fastest.
Arguments:
- user_feats: bfloat16 [24576, 2048], P('client'), may hold values from -6 to 6
- item_feats: bfloat16 [24576, 2048], P('client'), may hold values from -6 to 6
- item_ids: int32 [24576], P('client'), may hold values from 0 to 999
- picks: int32 [256], P('client'), may hold values from 0 to 15
- user_weight: bfloat16 [16, 2048, 512], P('cluster'), may hold values from -0.125 to 0.125
- item_weight: bfloat16 [16, 2048, 512], P('cluster'), may hold values from -0.125 to 0.125
Outputs:
- loss_table: float32 [256, 16], P('client')
- user_grad: float32 [16, 2048, 512], P('cluster', 'client')
- item_grad: float32 [16, 2048, 512], P('cluster', 'client')
The draws below stay inside these ranges and needn't reach their ends.
Inputs may be any that keep to these rules, and one draw needn't show every extreme that they name: `picks`: one cluster per client.
All inputs are finite; a program needn't handle non-finite values.
Results may differ from the reference program's by a relative error of at most 0.005.
Values sent between devices are 32-bit elements; how exact they have to be, the bound alone decides.
A program may use at most 128 MiB of HBM per device.

```python
import math
import jax
import jax.numpy as jnp
import numpy as np
from jax import lax

D = 2048
E = 512
R = 96
CLIENTS = 256
CLUSTERS = 16


def with_ends(entries, stream_key, least, top_value):
    longest = entries.shape.index(max(entries.shape))
    spots = []
    for shift in (0, 1):
        where = [jax.random.randint(jax.random.fold_in(stream_key, axis), (), 0, length) for axis, length in enumerate(entries.shape)]
        where[longest] = (where[longest] + shift) % entries.shape[longest]
        spots.append(tuple(where))
    return entries.at[spots[0]].set(least).at[spots[1]].set(top_value)


def raised(result, own_key, source, target, shards_of, factor):
    owner, partner = [(jnp.arange(result.shape[axis_at]) // (result.shape[axis_at] // shards_of)).reshape([-1 if axis == axis_at else 1 for axis in range(result.ndim)]) for axis_at in (source, target)]
    chosen = jax.random.permutation(own_key, shards_of)[partner]
    strong = (owner == chosen) | (owner == (partner + shards_of // 2) % shards_of)
    return jnp.where(strong, factor * result, result)


def block_scale(own_key, dims, shards, least, largest):
    def one(dim, parts):
        draws = jax.random.uniform(jax.random.fold_in(jax.random.fold_in(own_key, 6), dim), (parts,), jnp.float32, least / len(shards), largest / len(shards))
        return jnp.repeat(jnp.exp(draws), dims[dim] // parts).reshape((-1,) + (1,) * (len(dims) - dim - 1))

    factor_of = one(*shards[0])
    for cut in shards[1:]:
        factor_of = factor_of * one(*cut)
    return factor_of


def rank_bounds(count, lean):
    weights = [(1 << 20) // math.isqrt(standing ** lean) + 1 for standing in range(1, count + 1)]
    spread = 1 + sum(weights) // (1 << 30)
    return np.cumsum(np.array([max(1, weight // spread) for weight in weights]))


def ranked_ids(rng, extent, number_of, skew):
    listing = rank_bounds(number_of, skew)
    lot = jax.random.randint(jax.random.fold_in(rng, 1), extent, 0, int(listing[number_of - 1]))
    standing = jnp.searchsorted(jnp.asarray(listing, jnp.int32), lot, side="right")
    return jax.random.permutation(jax.random.fold_in(rng, 2), number_of)[standing].astype(jnp.int32)


def gaussian(own_key, shape, spread, reach, split=(), held_as=jnp.bfloat16):
    drawn = spread * jax.random.normal(own_key, shape, jnp.float32)
    if split:
        drawn = drawn * block_scale(own_key, shape, split, -0.22, 0.18)
    return jnp.clip(drawn, -reach, reach).astype(held_as)


def gaussian_with(stream_key, extent, width, reach, cuts, heavy, kind=jnp.bfloat16):
    array = width * jax.random.normal(stream_key, extent, jnp.float32)
    if cuts:
        array = array * block_scale(stream_key, extent, cuts, -0.22, 0.18)
    return jnp.clip(raised(array, jax.random.fold_in(stream_key, 3), *heavy), -reach, reach).astype(kind)


def setup_inputs(seed: int = 0) -> dict:
    arg_keys = jax.random.split(jax.random.key(seed), 7)
    user_feats = gaussian_with(arg_keys[0], (CLIENTS * R, D), 1.0, 6.0, ((0, 16),), (0, 1, 16, 2.0))
    item_feats = gaussian_with(arg_keys[1], (CLIENTS * R, D), 1.0, 6.0, ((0, 16),), (0, 1, 16, 2.0))
    item_ids = with_ends(ranked_ids(arg_keys[2], (CLIENTS * R,), 1000, 2), jax.random.fold_in(arg_keys[2], 3), 0, 999).astype(jnp.int32)
    picks = with_ends(ranked_ids(arg_keys[3], (CLIENTS,), CLUSTERS, 1), jax.random.fold_in(arg_keys[3], 3), 0, CLUSTERS - 1).astype(jnp.int32)
    user_weight = gaussian(arg_keys[4], (CLUSTERS, D, E), D ** -0.5, 0.125, ((0, 16),))
    item_weight = gaussian(arg_keys[5], (CLUSTERS, D, E), D ** -0.5, 0.125, ((0, 16),))
    return dict(user_feats=user_feats, item_feats=item_feats, item_ids=item_ids, picks=picks, user_weight=user_weight, item_weight=item_weight)


def silu_slope(pre_act):
    sig = jax.nn.sigmoid(pre_act)
    return sig * (1.0 + pre_act * (1.0 - sig))

def contract_rows(left, right):
    return lax.dot_general(left, right, (((0,), (0,)), ((), ())), preferred_element_type=jnp.float32)

def reference(user_feats, item_feats, item_ids, picks, user_weight, item_weight):
    temper = 1.0 / math.sqrt(E)
    grouped = item_ids.reshape(CLIENTS, R)
    labels = (grouped[:, :, None] == grouped[:, None, :]).astype(jnp.float32)

    def per_cluster(cluster_index):
        user_map = user_weight[cluster_index]
        item_map = item_weight[cluster_index]
        pre_user = jnp.dot(user_feats, user_map, preferred_element_type=jnp.float32)
        user_vec = jax.nn.silu(pre_user).astype(jnp.bfloat16)
        item_vec = jnp.dot(item_feats, item_map, preferred_element_type=jnp.float32).astype(jnp.bfloat16)
        user_blocks = lax.optimization_barrier(user_vec).astype(jnp.float32).reshape(CLIENTS, R, E)
        item_blocks = lax.optimization_barrier(item_vec).astype(jnp.float32).reshape(CLIENTS, R, E)
        scores = jnp.einsum('cre,cte->crt', user_blocks, item_blocks) * temper
        pair_loss = jax.nn.softplus(scores) - labels * scores
        client_loss = lax.optimization_barrier(jnp.mean(pair_loss, axis=(1, 2)))
        chosen = (picks == cluster_index).astype(jnp.float32)
        slope = ((jax.nn.sigmoid(scores) - labels) * temper * chosen[:, None, None]).astype(jnp.bfloat16)
        slope = lax.optimization_barrier(slope).astype(jnp.float32)
        user_slope = jnp.einsum('crt,cte->cre', slope, item_blocks).reshape(CLIENTS * R, E)
        pre_slope = (user_slope * silu_slope(pre_user)).astype(jnp.bfloat16)
        item_slope = jnp.einsum('crt,cre->cte', slope, user_blocks).reshape(CLIENTS * R, E).astype(jnp.bfloat16)
        grad_user = contract_rows(user_feats, pre_slope)
        grad_item = contract_rows(item_feats, item_slope)
        return (client_loss, grad_user, grad_item)
    losses, grad_user, grad_item = lax.map(per_cluster, jnp.arange(CLUSTERS, dtype=jnp.int32))
    return (losses.T, grad_user, grad_item)
```

```python
import functools
import math

import jax
import jax.numpy as jnp
from jax import lax
from jax.experimental import pallas as pl
from jax.experimental.pallas import tpu as pltpu
from jax.sharding import PartitionSpec as P

MESH = pl.DeviceIdType.MESH
NX = 4
ORDER = (2, 1, 3, 0)


def kernel(cfg, uf, itf, ids, picks, uw, iw, loss_out, ug_out, ig_out,
           fu, fi, wu, wi, pre, iv, uvec, pst, ist, gt, crecv, ya, yb,
           xa1, xal, xar, xb1, xbl, xbr, tile, table,
           ld, cs, cr, ys, yr, xs, xr, ls, lr):
    clients, rows, width, split, groups, clusters = cfg
    depth = fu.shape[1]
    per = clients // groups
    grp = per * rows
    temper = 1.0 / math.sqrt(width)
    k_me = lax.axis_index("cluster")
    s_me = lax.axis_index("client")
    x = s_me // 4
    y = (s_me // 2) % 2
    c = s_me % 2
    mate = {"client": x * 4 + y * 2 + (1 - c)}
    across = {"client": x * 4 + (1 - y) * 2 + c}
    right = {"client": ((x + 1) % NX) * 4 + y * 2 + c}
    left = {"client": ((x + NX - 1) % NX) * 4 + y * 2 + c}

    def load(src, dst, n):
        return pltpu.make_async_copy(src, dst, ld.at[n])

    load_wu = load(uw.at[0], wu, 0)
    load_wi = load(iw.at[0], wi, 1)
    load_u = [load(uf.at[pl.ds(g * grp, grp)], fu.at[pl.ds(g * grp, grp)], 2 + g) for g in range(groups)]
    load_i = [load(itf.at[pl.ds(g * grp, grp)], fi.at[pl.ds(g * grp, grp)], 2 + groups + g) for g in range(groups)]
    load_wu.start()
    load_u[0].start()
    load_wi.start()
    load_i[0].start()
    for g in range(1, groups):
        load_u[g].start()
        load_i[g].start()

    barrier = pltpu.get_barrier_semaphore()
    for peer in (mate, across, right, left):
        pl.semaphore_signal(barrier, inc=1, device_id=peer, device_id_type=MESH)
    for n in range(1, clusters):
        pl.semaphore_signal(barrier, inc=1, device_id={"cluster": (k_me + n) % clusters}, device_id_type=MESH)

    def towers(g):
        if g == 0:
            load_wu.wait()
        load_u[g].wait()
        pre[g % 2] = jnp.dot(fu[g * grp:(g + 1) * grp, :], wu[...], preferred_element_type=jnp.float32)
        if g == 0:
            load_wi.wait()
        load_i[g].wait()
        iv[g % 2] = jnp.dot(fi[g * grp:(g + 1) * grp, :], wi[...], preferred_element_type=jnp.float32).astype(jnp.bfloat16)

    def slopes(g):
        p = pre[g % 2]
        sig = 1.0 / (1.0 + jnp.exp(-p))
        uvec[...] = (p * sig).astype(jnp.bfloat16)
        pre[g % 2] = sig * (1.0 + p * (1.0 - sig))
        pres, items = [], []
        for n in range(per):
            client = g * per + n
            at = slice(n * rows, (n + 1) * rows)
            u = uvec[at, :]
            v = iv[g % 2, at, :]
            s = lax.dot_general(u, v, (((1,), (1,)), ((), ())), preferred_element_type=jnp.float32) * temper
            across_ids = jnp.broadcast_to(ids[pl.ds(client, 1), :], (rows, rows))
            labels = (across_ids == across_ids.T).astype(jnp.float32)
            tail = jnp.exp(-jnp.abs(s))
            pair = jnp.maximum(s, 0.0) + jnp.log(1.0 + tail) - labels * s
            mean = jnp.sum(pair, axis=(0, 1), keepdims=True) / (rows * rows)
            tile[pl.ds(client, 1), :] = jnp.broadcast_to(mean, (1, 128))
            gate = jnp.where(s >= 0.0, 1.0, tail) / (1.0 + tail)
            chosen = jnp.where(picks[client] == k_me, temper, 0.0).astype(jnp.float32)
            slope = ((gate - labels) * chosen).astype(jnp.bfloat16)
            us = jnp.dot(slope, v, preferred_element_type=jnp.float32)
            pres.append(us * pre[g % 2, at, :])
            items.append(lax.dot_general(slope, u, (((0,), (0,)), ((), ())), preferred_element_type=jnp.float32))
        pst[:, g * grp:(g + 1) * grp] = jnp.concatenate(pres, axis=0).T.astype(jnp.bfloat16)
        ist[:, g * grp:(g + 1) * grp] = jnp.concatenate(items, axis=0).T.astype(jnp.bfloat16)

    towers(0)
    for g in range(groups):
        if g + 1 < groups:
            towers(g + 1)
        slopes(g)

    pl.semaphore_wait(barrier, 4 + clusters - 1)

    table[pl.ds(k_me, 1)] = tile[...][None]
    loss_copies = []
    for n in range(1, clusters):
        copy = pltpu.make_async_remote_copy(
            src_ref=tile, dst_ref=table.at[k_me], send_sem=ls.at[n], recv_sem=lr.at[n],
            device_id={"cluster": (k_me + n) % clusters}, device_id_type=MESH)
        copy.start()
        loss_copies.append(copy)

    A = pl.ds(0, split)
    B = pl.ds(split, width - split)

    def step_of(dx, dy):
        return 2 * ORDER.index(dx) + (1 - dy)

    def own(dx, dy, t, part):
        return gt.at[step_of(dx, dy), t, c, part]

    def send(src, dst, ssem, rsem, peer):
        return pltpu.make_async_remote_copy(src_ref=src, dst_ref=dst, send_sem=ssem, recv_sem=rsem,
                                            device_id=peer, device_id_type=MESH)

    def core_copy(step, t):
        return send(gt.at[step, t, 1 - c], crecv.at[step, t], cs.at[step, t], cr.at[step, t], mate)

    def ya_copy(dx, t):
        return send(own(dx, 1, t, A), ya.at[dx, t], ys.at[dx, t], yr.at[dx, t], across)

    def yb_copy(t):
        return send(own(0, 1, t, B), yb.at[t], ys.at[4, t], yr.at[4, t], across)

    def x_part(which):
        return (0, A, xa1, xal, xar) if which == 2 else (which, B, xb1.at[which], xbl.at[which], xbr.at[which])

    def far_copy(which, t):
        dy, part, first, _, _ = x_part(which)
        return send(own(2, dy, t, part), first.at[t], xs.at[which, 0, t], xr.at[which, 0, t], (right, left)[t])

    def near_copy(which, t, rightward):
        dy, part, _, from_left, from_right = x_part(which)
        if rightward:
            return send(own(1, dy, t, part), from_left.at[t], xs.at[which, 1, t], xr.at[which, 1, t], right)
        return send(own(3, dy, t, part), from_right.at[t], xs.at[which, 2, t], xr.at[which, 2, t], left)

    def add(dst, src):
        dst[...] += src[...]

    def far_arrived(which, t):
        dy, part, first, _, _ = x_part(which)
        far_copy(which, t).wait_recv()
        add(own((1, 3)[t], dy, t, part), first.at[t])
        near_copy(which, t, t == 0).start()

    def near_arrived(which):
        dy, part, _, from_left, from_right = x_part(which)
        for t in (0, 1):
            near_copy(which, t, True).wait_recv()
            near_copy(which, t, False).wait_recv()
            mine = own(0, dy, t, part)
            mine[...] += from_left[t] + from_right[t]

    def ya_arrived(dx):
        for t in (0, 1):
            ya_copy(dx, t).wait_recv()
            add(own(dx, 0, t, A), ya.at[dx, t])

    def ready(step):
        dx, dy = ORDER[step // 2], 1 - step % 2
        for t in (0, 1):
            core_copy(step, t).wait_recv()
            mine = gt.at[step, t, c]
            mine[...] += crecv[step, t]
            if dx == 2:
                far_copy(dy, t).start()
            if dy == 1:
                ya_copy(dx, t).start()
            if dx == 1 and t == 1:
                near_copy(dy, 1, True).start()
            if dx == 3 and t == 0:
                near_copy(dy, 0, False).start()

    def body(step, carry):
        q = step // 2
        dx = (2 + 3 * q + 3 * (q * (q - 1) // 2)) % NX
        dy = 1 - step % 2
        chip = ((x + dx) % NX) * 2 + (y + dy) % 2
        cols = pl.ds(pl.multiple_of(chip * 256, 256), 256)
        for t, (left_t, feats) in enumerate(((pst, fu), (ist, fi))):
            r = jnp.dot(left_t[...], feats[:, cols], preferred_element_type=jnp.float32)
            gt[step, t, 0] = r[:, :128]
            gt[step, t, 1] = r[:, 128:]
            core_copy(step, t).start()
        for n in range(2 * NX - 1):
            @pl.when(step == n + 1)
            def _(n=n):
                ready(n)
                if n >= 3:
                    far_arrived(n % 2, (n - 3) // 2)
        return carry

    lax.fori_loop(0, 2 * NX, body, 0)
    ready(2 * NX - 1)
    ya_arrived(2)
    far_copy(2, 0).start()
    far_copy(2, 1).start()
    ya_arrived(1)
    near_copy(2, 1, True).start()
    ya_arrived(3)
    near_copy(2, 0, False).start()
    near_arrived(1)
    yb_copy(0).start()
    yb_copy(1).start()
    far_arrived(2, 0)
    far_arrived(2, 1)
    near_arrived(0)
    ya_arrived(0)

    for copy in loss_copies:
        copy.wait()
    lane = lax.broadcasted_iota(jnp.int32, (clients, 128), 1)
    total = jnp.zeros((clients, 128), jnp.float32)
    for n in range(clusters):
        total = total + jnp.where(lane == n, table[n], 0.0)
    loss_out[...] = total[:, :clusters]

    outs = (ug_out, ig_out)
    for t in (0, 1):
        yb_copy(t).wait_recv()
        res = gt[step_of(0, 0), t, c, split:, :] + yb[t]
        outs[t][0, :, split:] = res.T
    near_arrived(2)
    for t in (0, 1):
        outs[t][0, :, :split] = gt[step_of(0, 0), t, c, :split, :].T

    for step in range(2 * NX):
        for t in (0, 1):
            core_copy(step, t).wait_send()
    for t in (0, 1):
        for dx in range(NX):
            ya_copy(dx, t).wait_send()
        yb_copy(t).wait_send()
        for which in range(3):
            far_copy(which, t).wait_send()
            near_copy(which, t, True).wait_send()
            near_copy(which, t, False).wait_send()


def body(user_feats, item_feats, item_ids, picks, user_weight, item_weight):
    clients = picks.shape[0]
    total, depth = user_feats.shape
    rows = total // clients
    width = user_weight.shape[2]
    clusters = lax.axis_size("cluster")
    groups = 4
    grp = total // groups
    split = width * 7 // 16
    rest = width - split
    f32, bf16 = jnp.float32, jnp.bfloat16
    vmem = pltpu.VMEM
    dma = pltpu.SemaphoreType.DMA
    any_spec = pl.BlockSpec(memory_space=pl.ANY)
    vmem_spec = pl.BlockSpec(memory_space=pltpu.VMEM)
    smem_spec = pl.BlockSpec(memory_space=pltpu.SMEM)
    return pl.pallas_call(
        functools.partial(kernel, (clients, rows, width, split, groups, clusters)),
        out_shape=(
            jax.ShapeDtypeStruct((clients, clusters), f32),
            jax.ShapeDtypeStruct((1, depth // 16, width), f32),
            jax.ShapeDtypeStruct((1, depth // 16, width), f32),
        ),
        in_specs=[any_spec, any_spec, vmem_spec, smem_spec, any_spec, any_spec],
        out_specs=(vmem_spec, vmem_spec, vmem_spec),
        scratch_shapes=[
            vmem((total, depth), bf16), vmem((total, depth), bf16),
            vmem((depth, width), bf16), vmem((depth, width), bf16),
            vmem((2, grp, width), f32), vmem((2, grp, width), bf16), vmem((grp, width), bf16),
            vmem((width, total), bf16), vmem((width, total), bf16),
            vmem((8, 2, 2, width, 128), f32), vmem((8, 2, width, 128), f32),
            vmem((4, 2, split, 128), f32), vmem((2, rest, 128), f32),
            vmem((2, split, 128), f32), vmem((2, split, 128), f32), vmem((2, split, 128), f32),
            vmem((2, 2, rest, 128), f32), vmem((2, 2, rest, 128), f32), vmem((2, 2, rest, 128), f32),
            vmem((clients, 128), f32), vmem((clusters, clients, 128), f32),
            dma((2 + 2 * groups,)), dma((8, 2)), dma((8, 2)), dma((5, 2)), dma((5, 2)),
            dma((3, 3, 2)), dma((3, 3, 2)), dma((clusters,)), dma((clusters,)),
        ],
        compiler_params=pltpu.CompilerParams(
            collective_id=0, has_side_effects=True, vmem_limit_bytes=64 * 1024 * 1024 - 65536),
        name="round",
    )(user_feats, item_feats, item_ids.reshape(clients, rows), picks, user_weight, item_weight)


def solution(mesh):
    in_specs = (P("client", None), P("client", None), P("client"), P("client"),
                P("cluster", None, None), P("cluster", None, None))
    out_specs = (P("client", None), P("cluster", "client", None), P("cluster", "client", None))
    return jax.shard_map(body, mesh=mesh, in_specs=in_specs, out_specs=out_specs, check_vma=False)
```

```python
import functools
import math

import jax
import jax.numpy as jnp
from jax import lax
from jax.experimental import pallas as pl
from jax.experimental.pallas import tpu as pltpu
from jax.sharding import PartitionSpec as P

MESH = pl.DeviceIdType.MESH
NX = 4
VMEM_BYTES = 46 * 1024 * 1024
AHEAD = 3
ORDER = (2, 1, 3, 0)


def kernel(cfg, uf, itf, ids_hbm, picks_hbm, uw, iw, fin, table,
           ids, picks, fu, fi, wu, wi, pre, iv, uvec, pst, ist, gt, crecv, ya, yb,
           xa1, xal, xar, xb1, xbl, xbr,
           ld, cs, cr, ys, yr, xs, xr, ls, lr):
    clients, rows, width, split, groups, clusters = cfg
    depth = fu.shape[1]
    per = clients // groups
    grp = per * rows
    temper = 1.0 / math.sqrt(width)
    k_me = lax.axis_index("cluster")
    s_me = lax.axis_index("client")
    x = s_me // 4
    y = (s_me // 2) % 2
    c = s_me % 2
    mate = {"client": x * 4 + y * 2 + (1 - c)}
    across = {"client": x * 4 + (1 - y) * 2 + c}
    right = {"client": ((x + 1) % NX) * 4 + y * 2 + c}
    left = {"client": ((x + NX - 1) % NX) * 4 + y * 2 + c}
    nz = clusters // 2
    h = k_me // nz
    z = k_me % nz
    twin = {"cluster": (1 - h) * nz + z}
    above = {"cluster": h * nz + (z + 1) % nz}
    below = {"cluster": h * nz + (z + nz - 1) % nz}

    def load(src, dst, n):
        return pltpu.make_async_copy(src, dst, ld.at[n])

    load_wu = load(uw.at[0], wu, 0)
    load_wi = load(iw.at[0], wi, 1)
    load_u = [load(uf.at[pl.ds(g * grp, grp)], fu.at[pl.ds(g * grp, grp)], 2 + g) for g in range(groups)]
    load_i = [load(itf.at[pl.ds(g * grp, grp)], fi.at[pl.ds(g * grp, grp)], 2 + groups + g) for g in range(groups)]
    load_ids = load(ids_hbm, ids, 2 + 2 * groups)
    load_picks = load(picks_hbm, picks, 3 + 2 * groups)
    loads = [load_wu, load_u[0], load_wi, load_i[0]]
    for g in range(1, groups):
        loads += [load_u[g], load_i[g]]
    for copy in loads[:AHEAD]:
        copy.start()
    load_ids.start()
    load_picks.start()

    def arrive(copy):
        copy.wait()
        later = [load is copy for load in loads].index(True) + AHEAD
        if later < len(loads):
            loads[later].start()

    barrier = pltpu.get_barrier_semaphore()
    for peer in (mate, across, right, left, twin, above, below):
        pl.semaphore_signal(barrier, inc=1, device_id=peer, device_id_type=MESH)
    def towers(g):
        if g == 0:
            arrive(load_wu)
        arrive(load_u[g])
        pre[g % 2] = jnp.dot(fu[g * grp:(g + 1) * grp, :], wu[...], preferred_element_type=jnp.float32)
        if g == 0:
            arrive(load_wi)
        arrive(load_i[g])
        iv[g % 2] = jnp.dot(fi[g * grp:(g + 1) * grp, :], wi[...], preferred_element_type=jnp.float32).astype(jnp.bfloat16)

    lane8 = lax.broadcasted_iota(jnp.int32, (8, 128), 1)
    losses = [jnp.zeros((8, 128), jnp.float32)]

    def ids_of(g, n):
        first, off = divmod((g * per + n) * rows, 128)
        shape = (rows, 128)
        got = jnp.broadcast_to(ids[pl.ds(first, 1), :], shape)
        if off:
            got = pltpu.roll(got, 128 - off, 1)
        if off + rows > 128:
            more = pltpu.roll(jnp.broadcast_to(ids[pl.ds(first + 1, 1), :], shape), 128 - off, 1)
            got = jnp.where(lax.broadcasted_iota(jnp.int32, shape, 1) < 128 - off, got, more)
        return got[:, :rows]

    def slopes(g):
        if g == 0:
            load_ids.wait()
            load_picks.wait()
        p = pre[g % 2]
        sig = 1.0 / (1.0 + jnp.exp(-p))
        uvec[...] = (p * sig).astype(jnp.bfloat16)
        pre[g % 2] = sig * (1.0 + p * (1.0 - sig))
        pres, items = [], []
        for n in range(per):
            client = g * per + n
            at = slice(n * rows, (n + 1) * rows)
            u = uvec[at, :]
            v = iv[g % 2, at, :]
            s = lax.dot_general(u, v, (((1,), (1,)), ((), ())), preferred_element_type=jnp.float32) * temper
            across_ids = ids_of(g, n)
            labels = (across_ids == across_ids.T).astype(jnp.float32)
            tail = jnp.exp(-jnp.abs(s))
            pair = jnp.maximum(s, 0.0) + jnp.log(1.0 + tail) - labels * s
            mean = jnp.sum(pair, axis=(0, 1), keepdims=True) / (rows * rows)
            losses[0] = jnp.where(lane8 == client, mean, losses[0])
            gate = jnp.where(s >= 0.0, 1.0, tail) / (1.0 + tail)
            chosen = jnp.where(picks[client] == k_me, temper, 0.0).astype(jnp.float32)
            slope = ((gate - labels) * chosen).astype(jnp.bfloat16)
            us = jnp.dot(slope, v, preferred_element_type=jnp.float32)
            pres.append(us * pre[g % 2, at, :])
            items.append(lax.dot_general(slope, u, (((0,), (0,)), ((), ())), preferred_element_type=jnp.float32))
        pst[:, g * grp:(g + 1) * grp] = jnp.concatenate(pres, axis=0).T.astype(jnp.bfloat16)
        ist[:, g * grp:(g + 1) * grp] = jnp.concatenate(items, axis=0).T.astype(jnp.bfloat16)

    towers(0)
    for g in range(groups):
        if g + 1 < groups:
            towers(g + 1)
        slopes(g)

    pl.semaphore_wait(barrier, 7)

    def send(src, dst, ssem, rsem, peer):
        return pltpu.make_async_remote_copy(src_ref=src, dst_ref=dst, send_sem=ssem, recv_sem=rsem,
                                            device_id=peer, device_id_type=MESH)

    table[h, z] = losses[0]

    def twin_copy():
        return send(table.at[h, z], table.at[h, z], ls.at[0], lr.at[0], twin)

    def loss_copy(n, up):
        at = (z + (nz - n if up else n)) % nz
        part = table.at[:, pl.ds(at, 1)]
        sem = 1 + 2 * n + (0 if up else 1)
        return send(part, part, ls.at[sem], lr.at[sem], above if up else below)

    def loss_copies(n):
        return [loss_copy(n, True)] + ([loss_copy(n, False)] if n < nz // 2 - 1 else [])

    def loss_step(n):
        if n == 0:
            twin_copy().wait_recv()
        elif n <= nz // 2:
            for copy in loss_copies(n - 1):
                copy.wait_recv()
        if n < nz // 2:
            for copy in loss_copies(n):
                copy.start()

    twin_copy().start()

    A = pl.ds(0, split)
    B = pl.ds(split, width - split)

    def step_of(dx, dy):
        return 2 * ORDER.index(dx) + (1 - dy)

    def own(dx, dy, t, part):
        return gt.at[step_of(dx, dy), t, c, part]

    def core_copy(step, t):
        return send(gt.at[step, t, 1 - c], crecv.at[step, t], cs.at[step, t], cr.at[step, t], mate)

    def ya_copy(dx, t):
        return send(own(dx, 1, t, A), ya.at[dx, t], ys.at[dx, t], yr.at[dx, t], across)

    def yb_copy(t):
        return send(own(0, 1, t, B), yb.at[t], ys.at[4, t], yr.at[4, t], across)

    def x_part(which):
        return (0, A, xa1, xal, xar) if which == 2 else (which, B, xb1.at[which], xbl.at[which], xbr.at[which])

    def far_copy(which, t):
        dy, part, first, _, _ = x_part(which)
        return send(own(2, dy, t, part), first.at[t], xs.at[which, 0, t], xr.at[which, 0, t], (right, left)[t])

    def near_copy(which, t, rightward):
        dy, part, _, from_left, from_right = x_part(which)
        if rightward:
            return send(own(1, dy, t, part), from_left.at[t], xs.at[which, 1, t], xr.at[which, 1, t], right)
        return send(own(3, dy, t, part), from_right.at[t], xs.at[which, 2, t], xr.at[which, 2, t], left)

    def add(dst, src):
        dst[...] += src[...]

    def far_arrived(which, t):
        dy, part, first, _, _ = x_part(which)
        far_copy(which, t).wait_recv()
        add(own((1, 3)[t], dy, t, part), first.at[t])
        near_copy(which, t, t == 0).start()

    def near_arrived(which):
        dy, part, _, from_left, from_right = x_part(which)
        for t in (0, 1):
            near_copy(which, t, True).wait_recv()
            near_copy(which, t, False).wait_recv()
            mine = own(0, dy, t, part)
            mine[...] += from_left[t] + from_right[t]

    def ya_arrived(dx):
        for t in (0, 1):
            ya_copy(dx, t).wait_recv()
            add(own(dx, 0, t, A), ya.at[dx, t])

    def ready(step):
        dx, dy = ORDER[step // 2], 1 - step % 2
        for t in (0, 1):
            core_copy(step, t).wait_recv()
            mine = gt.at[step, t, c]
            mine[...] += crecv[step, t]
            if dx == 2:
                far_copy(dy, t).start()
            if dy == 1:
                ya_copy(dx, t).start()
            if dx == 1 and t == 1:
                near_copy(dy, 1, True).start()
            if dx == 3 and t == 0:
                near_copy(dy, 0, False).start()

    def body(step, carry):
        q = step // 2
        dx = (2 + 3 * q + 3 * (q * (q - 1) // 2)) % NX
        dy = 1 - step % 2
        chip = ((x + dx) % NX) * 2 + (y + dy) % 2
        cols = pl.ds(pl.multiple_of(chip * 256, 256), 256)
        for t, (left_t, feats) in enumerate(((pst, fu), (ist, fi))):
            r = jnp.dot(left_t[...], feats[:, cols], preferred_element_type=jnp.float32)
            gt[step, t, 0] = r[:, :128]
            gt[step, t, 1] = r[:, 128:]
            core_copy(step, t).start()
        for n in range(2 * NX - 1):
            @pl.when(step == n + 1)
            def _(n=n):
                ready(n)
                if n >= 1:
                    loss_step(n - 1)
                if n >= 5:
                    far_arrived(6 - n, 0)
                    far_arrived(6 - n, 1)
        return carry

    lax.fori_loop(0, 2 * NX, body, 0)
    ready(2 * NX - 1)
    ya_arrived(2)
    far_copy(2, 0).start()
    far_copy(2, 1).start()
    ya_arrived(1)
    near_copy(2, 1, True).start()
    ya_arrived(3)
    near_copy(2, 0, False).start()
    near_arrived(1)
    yb_copy(0).start()
    yb_copy(1).start()
    far_arrived(2, 0)
    far_arrived(2, 1)
    near_arrived(0)
    ya_arrived(0)

    for t in (0, 1):
        yb_copy(t).wait_recv()
        fin[t, split:, :] = gt[step_of(0, 0), t, c, split:, :] + yb[t]
    for t in (0, 1):
        near_copy(2, t, True).wait_recv()
        near_copy(2, t, False).wait_recv()
        fin[t, :split, :] = gt[step_of(0, 0), t, c, :split, :] + xal[t] + xar[t]

    twin_copy().wait_send()
    for n in range(nz // 2):
        for copy in loss_copies(n):
            copy.wait_send()
    for step in range(2 * NX):
        for t in (0, 1):
            core_copy(step, t).wait_send()
    for t in (0, 1):
        for dx in range(NX):
            ya_copy(dx, t).wait_send()
        yb_copy(t).wait_send()
        for which in range(3):
            far_copy(which, t).wait_send()
            near_copy(which, t, True).wait_send()
            near_copy(which, t, False).wait_send()


def finish(fin, table, loss_out, ug_out, ig_out):
    clients, clusters = loss_out.shape
    for t, out in enumerate((ug_out, ig_out)):
        out[0] = fin[t].T
    rows = table[...].reshape(clusters, 8, 128)[:, 0, :]
    loss_out[...] = rows.T[:clients, :]


def body(user_feats, item_feats, item_ids, picks, user_weight, item_weight):
    clients = picks.shape[0]
    total, depth = user_feats.shape
    rows = total // clients
    width = user_weight.shape[2]
    clusters = lax.axis_size("cluster")
    groups = 4
    grp = total // groups
    split = width * 7 // 16
    rest = width - split
    f32, bf16 = jnp.float32, jnp.bfloat16
    vmem = pltpu.VMEM
    dma = pltpu.SemaphoreType.DMA
    hbm_spec = pl.BlockSpec(memory_space=pltpu.HBM)
    vmem_spec = pl.BlockSpec(memory_space=pltpu.VMEM)
    fin, table = pl.pallas_call(
        functools.partial(kernel, (clients, rows, width, split, groups, clusters)),
        out_shape=(
            jax.ShapeDtypeStruct((2, width, 128), f32),
            jax.ShapeDtypeStruct((2, clusters // 2, 8, 128), f32),
        ),
        in_specs=[hbm_spec] * 6,
        out_specs=(vmem_spec, vmem_spec),
        scratch_shapes=[
            vmem((total // 128, 128), jnp.int32), pltpu.SMEM((clients,), jnp.int32),
            vmem((total, depth), bf16), vmem((total, depth), bf16),
            vmem((depth, width), bf16), vmem((depth, width), bf16),
            vmem((2, grp, width), f32), vmem((2, grp, width), bf16), vmem((grp, width), bf16),
            vmem((width, total), bf16), vmem((width, total), bf16),
            vmem((8, 2, 2, width, 128), f32), vmem((8, 2, width, 128), f32),
            vmem((4, 2, split, 128), f32), vmem((2, rest, 128), f32),
            vmem((2, split, 128), f32), vmem((2, split, 128), f32), vmem((2, split, 128), f32),
            vmem((2, 2, rest, 128), f32), vmem((2, 2, rest, 128), f32), vmem((2, 2, rest, 128), f32),
            dma((4 + 2 * groups,)), dma((8, 2)), dma((8, 2)), dma((5, 2)), dma((5, 2)),
            dma((3, 3, 2)), dma((3, 3, 2)), dma((clusters,)), dma((clusters,)),
        ],
        compiler_params=pltpu.CompilerParams(
            collective_id=0, has_side_effects=True, vmem_limit_bytes=VMEM_BYTES),
        name="round",
    )(*[pltpu.with_memory_space_constraint(a, pltpu.HBM) for a in (
        user_feats, item_feats, item_ids.reshape(total // 128, 128), picks, user_weight, item_weight)])
    return pl.pallas_call(
        finish,
        out_shape=(
            jax.ShapeDtypeStruct((clients, clusters), f32),
            jax.ShapeDtypeStruct((1, depth // 16, width), f32),
            jax.ShapeDtypeStruct((1, depth // 16, width), f32),
        ),
        in_specs=[vmem_spec, vmem_spec],
        out_specs=(vmem_spec, vmem_spec, vmem_spec),
        compiler_params=pltpu.CompilerParams(vmem_limit_bytes=8 * 1024 * 1024),
        name="finish",
    )(fin, table)


def solution(mesh):
    in_specs = (P("client", None), P("client", None), P("client"), P("client"),
                P("cluster", None, None), P("cluster", None, None))
    out_specs = (P("client", None), P("cluster", "client", None), P("cluster", "client", None))
    return jax.shard_map(body, mesh=mesh, in_specs=in_specs, out_specs=out_specs, check_vma=False)
```

```python
import functools
import math

import jax
import jax.numpy as jnp
from jax import lax
from jax.experimental import pallas as pl
from jax.experimental.pallas import tpu as pltpu
from jax.sharding import PartitionSpec as P

MESH = pl.DeviceIdType.MESH
NX = 4
ORDER = (2, 1, 3, 0)
PAIR = 2
PICKED_BYTES = 24 * 1024 * 1024
ROUND_BYTES = 46 * 1024 * 1024
FINISH_BYTES = 8 * 1024 * 1024
F32, BF16 = jnp.float32, jnp.bfloat16


def dot(a, b, dims=((1,), (0,))):
    return lax.dot_general(a, b, (dims, ((), ())), preferred_element_type=F32)


def same_item(ids, first, off, rows):
    shape = (rows, 128)
    last = ids.shape[0] - 1
    back = (128 - off) % 128
    got = pltpu.roll(jnp.broadcast_to(ids[pl.ds(first, 1), :], shape), back, 1)
    more = pltpu.roll(jnp.broadcast_to(ids[pl.ds(jnp.minimum(first + 1, last), 1), :], shape), back, 1)
    got = jnp.where(lax.broadcasted_iota(jnp.int32, shape, 1) < 128 - off, got, more)[:, :rows]
    return got == got.T


def picked(cfg, uf, itf, ids_hbm, picks_hbm, uw, iw, us_out, is_out,
           ids, picks, chosen, wu, wi, bu, bi, dsilu, uvec, iv, sem, bsem):
    clients, rows, width = cfg
    temper = 1.0 / math.sqrt(width)
    k_me = lax.axis_index("cluster")
    loads = [pltpu.make_async_copy(src, dst, sem.at[n]) for n, (src, dst) in enumerate(
        ((picks_hbm, picks), (uw.at[0], wu), (iw.at[0], wi), (ids_hbm, ids)))]
    for copy in loads:
        copy.start()
    loads[0].wait()

    def scan(client, count):
        chosen[count] = client
        return count + jnp.where(picks[client] == k_me, 1, 0)

    count = lax.fori_loop(0, clients, scan, 0)

    @pl.when(count % PAIR == 1)
    def _():
        chosen[count] = chosen[count - 1]

    pairs = (count + 1) // PAIR

    def fetch(p):
        slot = p % 2
        copies = []
        for n in range(PAIR):
            at = pl.ds(pl.multiple_of(chosen[PAIR * p + n] * rows, rows), rows)
            to = pl.ds(n * rows, rows)
            copies.append(pltpu.make_async_copy(uf.at[at], bu.at[slot, to], bsem.at[slot, 0, n]))
            copies.append(pltpu.make_async_copy(itf.at[at], bi.at[slot, to], bsem.at[slot, 1, n]))
        return copies

    @pl.when(pairs > 0)
    def _():
        for copy in fetch(0):
            copy.start()

    def clear(n, carry):
        at = pl.ds(pl.multiple_of(n * 64, 64), 64)
        us_out[at, :] = jnp.zeros((64, width), BF16)
        is_out[at, :] = jnp.zeros((64, width), BF16)
        return carry

    lax.fori_loop(0, clients * rows // 64, clear, 0)
    for copy in loads[1:]:
        copy.wait()

    def pair(p, carry):
        slot = p % 2

        @pl.when(p + 1 < pairs)
        def _():
            for copy in fetch(p + 1):
                copy.start()

        for copy in fetch(p):
            copy.wait()
        pre = dot(bu[slot], wu[...])
        sig = 0.5 * jnp.tanh(0.5 * pre) + 0.5
        u = pre * sig
        uvec[...] = u.astype(BF16)
        dsilu[...] = sig + (u - u * sig)
        iv[...] = dot(bi[slot], wi[...]).astype(BF16)
        for n in range(PAIR):
            client = chosen[PAIR * p + n]
            at = slice(n * rows, (n + 1) * rows)
            u = uvec[at, :]
            v = iv[at, :]
            s = dot(u, v, ((1,), (1,))) * temper
            start = client * rows
            same = same_item(ids, start // 128, start % 128, rows)
            gate = 0.5 * jnp.tanh(0.5 * s) + 0.5
            slope = (jnp.where(same, gate - 1.0, gate) * temper).astype(BF16)
            to = pl.ds(pl.multiple_of(start, rows), rows)
            us_out[to, :] = (dot(slope, v) * dsilu[at, :]).astype(BF16)
            is_out[to, :] = dot(slope, u, ((0,), (0,))).astype(BF16)
        return carry

    lax.fori_loop(0, pairs, pair, 0)


def kernel(cfg, uf, itf, ids_hbm, uw, iw, us, its, fin, table,
           ids, fu, fi, wu, wi, iv, uvec, gt, crecv, ya, yb,
           xa1, xal, xar, xb1, xbl, xbr,
           ld, cs, cr, ys, yr, xs, xr, ls, lr):
    clients, rows, width, split, groups, clusters = cfg
    total, depth = fu.shape
    per = clients // groups
    grp = per * rows
    temper = 1.0 / math.sqrt(width)
    k_me = lax.axis_index("cluster")
    s_me = lax.axis_index("client")
    x = s_me // 4
    y = (s_me // 2) % 2
    c = s_me % 2
    mate = {"client": x * 4 + y * 2 + (1 - c)}
    across = {"client": x * 4 + (1 - y) * 2 + c}
    right = {"client": ((x + 1) % NX) * 4 + y * 2 + c}
    left = {"client": ((x + NX - 1) % NX) * 4 + y * 2 + c}

    barrier = pltpu.get_barrier_semaphore()
    for peer in (mate, across, right, left):
        pl.semaphore_signal(barrier, inc=1, device_id=peer, device_id_type=MESH)
    for n in range(1, clusters):
        pl.semaphore_signal(barrier, inc=1, device_id={"cluster": (k_me + n) % clusters}, device_id_type=MESH)

    def columns(step):
        q = step // 2
        dx = (2 + 3 * q + 3 * (q * (q - 1) // 2)) % NX
        dy = 1 - step % 2
        chip = ((x + dx) % NX) * 2 + (y + dy) % 2
        return pl.ds(pl.multiple_of(chip * 256, 256), 256)

    def feats(step, t):
        src, dst = ((uf, fu), (itf, fi))[t]
        at = columns(step)
        return pltpu.make_async_copy(src.at[:, at], dst.at[:, at], ld.at[step, t])

    rest_loads = [pltpu.make_async_copy(src, dst, ld.at[2 * NX, n]) for n, (src, dst) in enumerate(
        ((uw.at[0], wu), (iw.at[0], wi), (ids_hbm, ids)))]
    for step in range(2):
        for t in (0, 1):
            feats(step, t).start()

    A = pl.ds(0, split)
    B = pl.ds(split, 128 - split)

    def step_of(dx, dy):
        return 2 * ORDER.index(dx) + (1 - dy)

    def own(dx, dy, t, part):
        return gt.at[step_of(dx, dy), t, c, part]

    def send(src, dst, ssem, rsem, peer):
        return pltpu.make_async_remote_copy(src_ref=src, dst_ref=dst, send_sem=ssem, recv_sem=rsem,
                                            device_id=peer, device_id_type=MESH)

    def loss_copy(n):
        return send(table.at[k_me], table.at[k_me], ls.at[n], lr.at[n], {"cluster": (k_me + n) % clusters})

    def core_copy(step, t):
        return send(gt.at[step, t, 1 - c], crecv.at[step, t], cs.at[step, t], cr.at[step, t], mate)

    def ya_copy(dx, t):
        return send(own(dx, 1, t, A), ya.at[dx, t], ys.at[dx, t], yr.at[dx, t], across)

    def yb_copy(t):
        return send(own(0, 1, t, B), yb.at[t], ys.at[4, t], yr.at[4, t], across)

    def x_part(which):
        return (0, A, xa1, xal, xar) if which == 2 else (which, B, xb1.at[which], xbl.at[which], xbr.at[which])

    def far_copy(which, t):
        dy, part, first, _, _ = x_part(which)
        return send(own(2, dy, t, part), first.at[t], xs.at[which, 0, t], xr.at[which, 0, t], (right, left)[t])

    def near_copy(which, t, rightward):
        dy, part, _, from_left, from_right = x_part(which)
        if rightward:
            return send(own(1, dy, t, part), from_left.at[t], xs.at[which, 1, t], xr.at[which, 1, t], right)
        return send(own(3, dy, t, part), from_right.at[t], xs.at[which, 2, t], xr.at[which, 2, t], left)

    def add(dst, src):
        dst[...] += src[...]

    def far_arrived(which, t):
        dy, part, first, _, _ = x_part(which)
        far_copy(which, t).wait_recv()
        add(own((1, 3)[t], dy, t, part), first.at[t])
        near_copy(which, t, t == 0).start()

    def near_arrived(which):
        dy, part, _, from_left, from_right = x_part(which)
        for t in (0, 1):
            near_copy(which, t, True).wait_recv()
            near_copy(which, t, False).wait_recv()
            mine = own(0, dy, t, part)
            mine[...] += from_left[t] + from_right[t]

    def ya_arrived(dx):
        for t in (0, 1):
            ya_copy(dx, t).wait_recv()
            add(own(dx, 0, t, A), ya.at[dx, t])

    def ready(step):
        dx, dy = ORDER[step // 2], 1 - step % 2
        for t in (0, 1):
            core_copy(step, t).wait_recv()
            mine = gt.at[step, t, c]
            mine[...] += crecv[step, t]
            if dx == 2:
                far_copy(dy, t).start()
            if dy == 1:
                ya_copy(dx, t).start()
            if dx == 1 and t == 1:
                near_copy(dy, 1, True).start()
            if dx == 3 and t == 0:
                near_copy(dy, 0, False).start()

    def blocks(step, carry):
        @pl.when(step + 2 < 2 * NX)
        def _():
            for t in (0, 1):
                feats(step + 2, t).start()

        @pl.when(step + 2 == 2 * NX)
        def _():
            for copy in rest_loads:
                copy.start()

        for t, (slope, feat) in enumerate(((us, fu), (its, fi))):
            feats(step, t).wait()
            r = dot(feat[:, columns(step)], slope[...], ((0,), (0,)))
            gt[step, t, 0] = r[:128]
            gt[step, t, 1] = r[128:]
            if t == 0:
                @pl.when(step == 0)
                def _():
                    pl.semaphore_wait(barrier, 4 + clusters - 1)
            core_copy(step, t).start()
        for n in range(2 * NX - 1):
            @pl.when(step == n + 1)
            def _(n=n):
                ready(n)
                if n >= 5:
                    far_arrived(6 - n, 0)
                    far_arrived(6 - n, 1)
        return carry

    lax.fori_loop(0, 2 * NX, blocks, 0)
    ready(2 * NX - 1)
    for copy in rest_loads:
        copy.wait()

    lane = lax.broadcasted_iota(jnp.int32, (1, 128), 1)

    def losses_of(g, losses):
        at = pl.ds(pl.multiple_of(g * grp, grp), grp)
        pre = dot(fu[at, :], wu[...])
        uvec[...] = (pre * (0.5 * jnp.tanh(0.5 * pre) + 0.5)).astype(BF16)
        iv[...] = dot(fi[at, :], wi[...]).astype(BF16)
        for n in range(per):
            rows_n = slice(n * rows, (n + 1) * rows)
            s = dot(uvec[rows_n, :], iv[rows_n, :], ((1,), (1,))) * temper
            first, off = divmod(n * rows, 128)
            same = same_item(ids, g * (grp // 128) + first, off, rows)
            pair = jnp.maximum(s, 0.0) + jnp.log(1.0 + jnp.exp(-jnp.abs(s))) - jnp.where(same, s, 0.0)
            mean = jnp.sum(pair, axis=(0, 1), keepdims=True) * (1.0 / (rows * rows))
            losses = jnp.where(lane == g * per + n, mean, losses)

        @pl.when(g == 0)
        def _():
            ya_arrived(2)
            far_copy(2, 0).start()
            far_copy(2, 1).start()

        @pl.when(g == 1)
        def _():
            ya_arrived(1)
            near_copy(2, 1, True).start()

        return losses

    losses = lax.fori_loop(0, groups, losses_of, jnp.zeros((1, 128), F32))
    table[k_me] = losses
    ya_arrived(3)
    near_copy(2, 0, False).start()
    for n in range(1, clusters):
        loss_copy(n).start()
    near_arrived(1)
    yb_copy(0).start()
    yb_copy(1).start()
    far_arrived(2, 0)
    far_arrived(2, 1)
    near_arrived(0)
    ya_arrived(0)

    for n in range(1, clusters):
        loss_copy(n).wait()
    for t in (0, 1):
        yb_copy(t).wait_recv()
        fin[t, split:, :] = gt[step_of(0, 0), t, c, split:, :] + yb[t]
    for t in (0, 1):
        near_copy(2, t, True).wait_recv()
        near_copy(2, t, False).wait_recv()
        fin[t, :split, :] = gt[step_of(0, 0), t, c, :split, :] + xal[t] + xar[t]

    for step in range(2 * NX):
        for t in (0, 1):
            core_copy(step, t).wait_send()
    for t in (0, 1):
        for dx in range(NX):
            ya_copy(dx, t).wait_send()
        yb_copy(t).wait_send()
        for which in range(3):
            far_copy(which, t).wait_send()
            near_copy(which, t, True).wait_send()
            near_copy(which, t, False).wait_send()


def finish(fin, table, loss_out, ug_out, ig_out):
    clients, clusters = loss_out.shape
    ug_out[0] = fin[0]
    ig_out[0] = fin[1]
    loss_out[...] = table[:, 0, :].T[:clients, :]


def body(user_feats, item_feats, item_ids, picks, user_weight, item_weight):
    clients = picks.shape[0]
    total, depth = user_feats.shape
    rows = total // clients
    width = user_weight.shape[2]
    clusters = lax.axis_size("cluster")
    groups = 4
    grp = total // groups
    split = 56
    rest = 128 - split
    vmem = pltpu.VMEM
    dma = pltpu.SemaphoreType.DMA
    hbm_spec = pl.BlockSpec(memory_space=pltpu.HBM)
    vmem_spec = pl.BlockSpec(memory_space=pltpu.VMEM)
    uf, itf, ids, picks, uw, iw = [pltpu.with_memory_space_constraint(a, pltpu.HBM) for a in (
        user_feats, item_feats, item_ids.reshape(total // 128, 128), picks, user_weight, item_weight)]
    us, its = pl.pallas_call(
        functools.partial(picked, (clients, rows, width)),
        out_shape=(jax.ShapeDtypeStruct((total, width), BF16), jax.ShapeDtypeStruct((total, width), BF16)),
        in_specs=[hbm_spec] * 6,
        out_specs=(vmem_spec, vmem_spec),
        scratch_shapes=[
            vmem((total // 128, 128), jnp.int32), pltpu.SMEM((clients,), jnp.int32), pltpu.SMEM((clients,), jnp.int32),
            vmem((depth, width), BF16), vmem((depth, width), BF16),
            vmem((2, PAIR * rows, depth), BF16), vmem((2, PAIR * rows, depth), BF16),
            vmem((PAIR * rows, width), F32), vmem((PAIR * rows, width), BF16), vmem((PAIR * rows, width), BF16),
            dma((4,)), dma((2, 2, PAIR)),
        ],
        compiler_params=pltpu.CompilerParams(vmem_limit_bytes=PICKED_BYTES),
        name="picked",
    )(uf, itf, ids, picks, uw, iw)
    fin, table = pl.pallas_call(
        functools.partial(kernel, (clients, rows, width, split, groups, clusters)),
        out_shape=(jax.ShapeDtypeStruct((2, 128, width), F32), jax.ShapeDtypeStruct((clusters, 1, 128), F32)),
        in_specs=[hbm_spec] * 5 + [vmem_spec] * 2,
        out_specs=(vmem_spec, vmem_spec),
        scratch_shapes=[
            vmem((total // 128, 128), jnp.int32),
            vmem((total, depth), BF16), vmem((total, depth), BF16),
            vmem((depth, width), BF16), vmem((depth, width), BF16),
            vmem((grp, width), BF16), vmem((grp, width), BF16),
            vmem((8, 2, 2, 128, width), F32), vmem((8, 2, 128, width), F32),
            vmem((4, 2, split, width), F32), vmem((2, rest, width), F32),
            vmem((2, split, width), F32), vmem((2, split, width), F32), vmem((2, split, width), F32),
            vmem((2, 2, rest, width), F32), vmem((2, 2, rest, width), F32), vmem((2, 2, rest, width), F32),
            dma((2 * NX + 1, 3)), dma((8, 2)), dma((8, 2)), dma((5, 2)), dma((5, 2)),
            dma((3, 3, 2)), dma((3, 3, 2)), dma((clusters,)), dma((clusters,)),
        ],
        compiler_params=pltpu.CompilerParams(
            collective_id=0, has_side_effects=True, vmem_limit_bytes=ROUND_BYTES),
        name="round",
    )(uf, itf, ids, uw, iw, us, its)
    return pl.pallas_call(
        finish,
        out_shape=(
            jax.ShapeDtypeStruct((clients, clusters), F32),
            jax.ShapeDtypeStruct((1, depth // 16, width), F32),
            jax.ShapeDtypeStruct((1, depth // 16, width), F32),
        ),
        in_specs=[vmem_spec, vmem_spec],
        out_specs=(vmem_spec, vmem_spec, vmem_spec),
        compiler_params=pltpu.CompilerParams(vmem_limit_bytes=FINISH_BYTES),
        name="finish",
    )(fin, table)


def solution(mesh):
    in_specs = (P("client", None), P("client", None), P("client"), P("client"),
                P("cluster", None, None), P("cluster", None, None))
    out_specs = (P("client", None), P("cluster", "client", None), P("cluster", "client", None))
    return jax.shard_map(body, mesh=mesh, in_specs=in_specs, out_specs=out_specs, check_vma=False)
```

```python
import functools
import math

import jax
import jax.numpy as jnp
from jax import lax
from jax.experimental import pallas as pl
from jax.experimental.pallas import tpu as pltpu
from jax.sharding import PartitionSpec as P

MESH = pl.DeviceIdType.MESH
NX = 4
ORDER = (2, 1, 3, 0)
PAIR = 2
PICKED_BYTES = 24 * 1024 * 1024
ROUND_BYTES = 46 * 1024 * 1024
FINISH_BYTES = 8 * 1024 * 1024
F32, BF16 = jnp.float32, jnp.bfloat16


def dot(a, b, dims=((1,), (0,))):
    return lax.dot_general(a, b, (dims, ((), ())), preferred_element_type=F32)


def same_item(ids, first, off, rows):
    shape = (rows, 128)
    last = ids.shape[0] - 1
    back = (128 - off) % 128
    got = pltpu.roll(jnp.broadcast_to(ids[pl.ds(first, 1), :], shape), back, 1)
    more = pltpu.roll(jnp.broadcast_to(ids[pl.ds(jnp.minimum(first + 1, last), 1), :], shape), back, 1)
    got = jnp.where(lax.broadcasted_iota(jnp.int32, shape, 1) < 128 - off, got, more)[:, :rows]
    return got == got.T


def columns(s_me, step):
    q = step // 2
    dx = (2 + 3 * q + 3 * (q * (q - 1) // 2)) % NX
    dy = 1 - step % 2
    chip = ((s_me // 4 + dx) % NX) * 2 + ((s_me // 2) % 2 + dy) % 2
    return pl.ds(pl.multiple_of(chip * 256, 256), 256)


def picked(cfg, uf, itf, ids_hbm, picks_hbm, uw, iw, us_out, is_out, cu_out, ci_out,
           ids, picks, chosen, wu, wi, bu, bi, dsilu, uvec, iv, sem, bsem):
    clients, rows, width = cfg
    temper = 1.0 / math.sqrt(width)
    k_me = lax.axis_index("cluster")
    loads = [pltpu.make_async_copy(src, dst, sem.at[n]) for n, (src, dst) in enumerate(
        ((picks_hbm, picks), (uw.at[0], wu), (iw.at[0], wi), (ids_hbm, ids)))]
    for copy in loads:
        copy.start()
    loads[0].wait()

    def scan(client, count):
        chosen[count] = client
        return count + jnp.where(picks[client] == k_me, 1, 0)

    count = lax.fori_loop(0, clients, scan, 0)

    @pl.when(count % PAIR == 1)
    def _():
        chosen[count] = chosen[count - 1]

    pairs = (count + 1) // PAIR

    def fetch(p):
        slot = p % 2
        copies = []
        for n in range(PAIR):
            at = pl.ds(pl.multiple_of(chosen[PAIR * p + n] * rows, rows), rows)
            to = pl.ds(n * rows, rows)
            copies.append(pltpu.make_async_copy(uf.at[at], bu.at[slot, to], bsem.at[slot, 0, n]))
            copies.append(pltpu.make_async_copy(itf.at[at], bi.at[slot, to], bsem.at[slot, 1, n]))
        return copies

    @pl.when(pairs > 0)
    def _():
        for copy in fetch(0):
            copy.start()

    def clear(n, carry):
        at = pl.ds(pl.multiple_of(n * 64, 64), 64)
        us_out[at, :] = jnp.zeros((64, width), BF16)
        is_out[at, :] = jnp.zeros((64, width), BF16)
        return carry

    first = columns(lax.axis_index("client"), 0)
    ahead = [pltpu.make_async_copy(src.at[:, first], dst, sem.at[4 + t])
             for t, (src, dst) in enumerate(((uf, cu_out), (itf, ci_out)))]
    for copy in ahead:
        copy.start()
    lax.fori_loop(0, clients * rows // 64, clear, 0)
    for copy in loads[1:]:
        copy.wait()

    def pair(p, carry):
        slot = p % 2

        @pl.when(p + 1 < pairs)
        def _():
            for copy in fetch(p + 1):
                copy.start()

        for copy in fetch(p):
            copy.wait()
        pre = dot(bu[slot], wu[...])
        sig = 0.5 * jnp.tanh(0.5 * pre) + 0.5
        u = pre * sig
        uvec[...] = u.astype(BF16)
        dsilu[...] = sig + (u - u * sig)
        iv[...] = dot(bi[slot], wi[...]).astype(BF16)
        for n in range(PAIR):
            client = chosen[PAIR * p + n]
            at = slice(n * rows, (n + 1) * rows)
            u = uvec[at, :]
            v = iv[at, :]
            s = dot(u, v, ((1,), (1,))) * temper
            start = client * rows
            same = same_item(ids, start // 128, start % 128, rows)
            gate = 0.5 * jnp.tanh(0.5 * s) + 0.5
            slope = (jnp.where(same, gate - 1.0, gate) * temper).astype(BF16)
            to = pl.ds(pl.multiple_of(start, rows), rows)
            us_out[to, :] = (dot(slope, v) * dsilu[at, :]).astype(BF16)
            is_out[to, :] = dot(slope, u, ((0,), (0,))).astype(BF16)
        return carry

    lax.fori_loop(0, pairs, pair, 0)
    for copy in ahead:
        copy.wait()


def kernel(cfg, uf, itf, ids_hbm, uw, iw, us, its, cu, ci, fin, table,
           ids, fu, fi, wu, wi, iv, uvec, gt, crecv, ya, yb,
           xa1, xal, xar, xb1, xbl, xbr,
           ld, cs, cr, ys, yr, xs, xr, ls, lr):
    clients, rows, width, split, groups, clusters = cfg
    total, depth = fu.shape
    per = clients // groups
    grp = per * rows
    temper = 1.0 / math.sqrt(width)
    k_me = lax.axis_index("cluster")
    s_me = lax.axis_index("client")
    x = s_me // 4
    y = (s_me // 2) % 2
    c = s_me % 2
    mate = {"client": x * 4 + y * 2 + (1 - c)}
    across = {"client": x * 4 + (1 - y) * 2 + c}
    right = {"client": ((x + 1) % NX) * 4 + y * 2 + c}
    left = {"client": ((x + NX - 1) % NX) * 4 + y * 2 + c}
    nz = clusters // 2
    h = k_me // nz
    z = k_me % nz
    twin = {"cluster": (1 - h) * nz + z}
    above = {"cluster": h * nz + (z + 1) % nz}
    below = {"cluster": h * nz + (z + nz - 1) % nz}

    barrier = pltpu.get_barrier_semaphore()
    for peer in (mate, across, right, left, twin, above, below):
        pl.semaphore_signal(barrier, inc=1, device_id=peer, device_id_type=MESH)

    def feats(step, t):
        src, dst = ((uf, fu), (itf, fi))[t]
        at = columns(s_me, step)
        return pltpu.make_async_copy(src.at[:, at], dst.at[:, at], ld.at[step, t])

    rest_loads = [pltpu.make_async_copy(src, dst, ld.at[2 * NX, n]) for n, (src, dst) in enumerate(
        ((uw.at[0], wu), (iw.at[0], wi), (ids_hbm, ids)))]
    for step in (1, 2):
        for t in (0, 1):
            feats(step, t).start()

    A = pl.ds(0, split)
    B = pl.ds(split, 128 - split)

    def step_of(dx, dy):
        return 2 * ORDER.index(dx) + (1 - dy)

    def own(dx, dy, t, part):
        return gt.at[step_of(dx, dy), t, c, part]

    def send(src, dst, ssem, rsem, peer):
        return pltpu.make_async_remote_copy(src_ref=src, dst_ref=dst, send_sem=ssem, recv_sem=rsem,
                                            device_id=peer, device_id_type=MESH)

    def twin_copy():
        return send(table.at[h, z], table.at[h, z], ls.at[0], lr.at[0], twin)

    def loss_copy(n, up):
        part = table.at[:, pl.ds((z + (nz - n if up else n)) % nz, 1)]
        sem = 1 + 2 * n + (0 if up else 1)
        return send(part, part, ls.at[sem], lr.at[sem], above if up else below)

    def loss_copies(n):
        return [loss_copy(n, True)] + ([loss_copy(n, False)] if n < nz // 2 - 1 else [])

    def loss_step(n):
        if n == 0:
            twin_copy().wait_recv()
        else:
            for copy in loss_copies(n - 1):
                copy.wait_recv()
        if n < nz // 2:
            for copy in loss_copies(n):
                copy.start()

    def core_copy(step, t):
        return send(gt.at[step, t, 1 - c], crecv.at[step, t], cs.at[step, t], cr.at[step, t], mate)

    def ya_copy(dx, t):
        return send(own(dx, 1, t, A), ya.at[dx, t], ys.at[dx, t], yr.at[dx, t], across)

    def yb_copy(t):
        return send(own(0, 1, t, B), yb.at[t], ys.at[4, t], yr.at[4, t], across)

    def x_part(which):
        return (0, A, xa1, xal, xar) if which == 2 else (which, B, xb1.at[which], xbl.at[which], xbr.at[which])

    def far_copy(which, t):
        dy, part, first, _, _ = x_part(which)
        return send(own(2, dy, t, part), first.at[t], xs.at[which, 0, t], xr.at[which, 0, t], (right, left)[t])

    def near_copy(which, t, rightward):
        dy, part, _, from_left, from_right = x_part(which)
        if rightward:
            return send(own(1, dy, t, part), from_left.at[t], xs.at[which, 1, t], xr.at[which, 1, t], right)
        return send(own(3, dy, t, part), from_right.at[t], xs.at[which, 2, t], xr.at[which, 2, t], left)

    def add(dst, src):
        dst[...] += src[...]

    def far_arrived(which, t):
        dy, part, first, _, _ = x_part(which)
        far_copy(which, t).wait_recv()
        add(own((1, 3)[t], dy, t, part), first.at[t])
        near_copy(which, t, t == 0).start()

    def near_arrived(which):
        dy, part, _, from_left, from_right = x_part(which)
        for t in (0, 1):
            near_copy(which, t, True).wait_recv()
            near_copy(which, t, False).wait_recv()
            mine = own(0, dy, t, part)
            mine[...] += from_left[t] + from_right[t]

    def ya_arrived(dx):
        for t in (0, 1):
            ya_copy(dx, t).wait_recv()
            add(own(dx, 0, t, A), ya.at[dx, t])

    def ready(step):
        dx, dy = ORDER[step // 2], 1 - step % 2
        for t in (0, 1):
            core_copy(step, t).wait_recv()
            mine = gt.at[step, t, c]
            mine[...] += crecv[step, t]
            if dx == 2:
                far_copy(dy, t).start()
            if dy == 1:
                ya_copy(dx, t).start()
            if dx == 1 and t == 1:
                near_copy(dy, 1, True).start()
            if dx == 3 and t == 0:
                near_copy(dy, 0, False).start()

    def block(step, lhs):
        for t, (slope, feat) in enumerate(((us, lhs[0]), (its, lhs[1]))):
            r = dot(feat(), slope[...], ((0,), (0,)))
            gt[step, t, 0] = r[:128]
            gt[step, t, 1] = r[128:]
            if isinstance(step, int) and step == 0 and t == 0:
                pl.semaphore_wait(barrier, 7)
            core_copy(step, t).start()

    def loaded(step):
        def of(t, buf):
            feats(step, t).wait()
            return buf[:, columns(s_me, step)]
        return functools.partial(of, 0, fu), functools.partial(of, 1, fi)

    def blocks(step, carry):
        @pl.when(step + 2 < 2 * NX)
        def _():
            for t in (0, 1):
                feats(step + 2, t).start()

        @pl.when(step == 2 * NX - 3)
        def _():
            for copy in rest_loads:
                copy.start()
            for t in (0, 1):
                feats(0, t).start()

        block(step, loaded(step))
        for n in range(2 * NX - 2):
            @pl.when(step == n + 1)
            def _(n=n):
                ready(n)
                if n == 5:
                    far_arrived(1, 0)
                    far_arrived(1, 1)
        return carry

    block(0, (lambda: cu[...], lambda: ci[...]))
    lax.fori_loop(1, 2 * NX - 1, blocks, 0)
    ready(2 * NX - 2)
    far_arrived(0, 0)
    far_arrived(0, 1)
    for copy in rest_loads:
        copy.wait()
    for t in (0, 1):
        feats(0, t).wait()
        feats(2 * NX - 1, t).wait()

    lane = lax.broadcasted_iota(jnp.int32, (1, 128), 1)

    def losses_of(g, losses):
        at = pl.ds(pl.multiple_of(g * grp, grp), grp)
        pre = dot(fu[at, :], wu[...])
        uvec[...] = (pre * (0.5 * jnp.tanh(0.5 * pre) + 0.5)).astype(BF16)
        iv[...] = dot(fi[at, :], wi[...]).astype(BF16)
        for n in range(per):
            rows_n = slice(n * rows, (n + 1) * rows)
            s = dot(uvec[rows_n, :], iv[rows_n, :], ((1,), (1,))) * temper
            first, off = divmod(n * rows, 128)
            same = same_item(ids, g * (grp // 128) + first, off, rows)
            pair = jnp.maximum(s, 0.0) + jnp.log(1.0 + jnp.exp(-jnp.abs(s))) - jnp.where(same, s, 0.0)
            mean = jnp.sum(pair, axis=(0, 1), keepdims=True) * (1.0 / (rows * rows))
            losses = jnp.where(lane == g * per + n, mean, losses)

        @pl.when(g == 0)
        def _():
            ya_arrived(2)
            far_copy(2, 0).start()
            far_copy(2, 1).start()

        @pl.when(g == 1)
        def _():
            ya_arrived(1)
            near_copy(2, 1, True).start()

        return losses

    losses = lax.fori_loop(0, groups, losses_of, jnp.zeros((1, 128), F32))
    table[h, z] = losses
    twin_copy().start()
    block(2 * NX - 1, (lambda: fu[:, columns(s_me, 2 * NX - 1)], lambda: fi[:, columns(s_me, 2 * NX - 1)]))
    ya_arrived(3)
    near_copy(2, 0, False).start()
    loss_step(0)
    near_arrived(1)
    yb_copy(0).start()
    yb_copy(1).start()
    ready(2 * NX - 1)
    loss_step(1)
    far_arrived(2, 0)
    far_arrived(2, 1)
    near_arrived(0)
    ya_arrived(0)
    loss_step(2)
    loss_step(3)
    for t in (0, 1):
        yb_copy(t).wait_recv()
        fin[t, split:, :] = gt[step_of(0, 0), t, c, split:, :] + yb[t]
    for t in (0, 1):
        near_copy(2, t, True).wait_recv()
        near_copy(2, t, False).wait_recv()
        fin[t, :split, :] = gt[step_of(0, 0), t, c, :split, :] + xal[t] + xar[t]
    loss_step(4)

    twin_copy().wait_send()
    for n in range(nz // 2):
        for copy in loss_copies(n):
            copy.wait_send()
    for step in range(2 * NX):
        for t in (0, 1):
            core_copy(step, t).wait_send()
    for t in (0, 1):
        for dx in range(NX):
            ya_copy(dx, t).wait_send()
        yb_copy(t).wait_send()
        for which in range(3):
            far_copy(which, t).wait_send()
            near_copy(which, t, True).wait_send()
            near_copy(which, t, False).wait_send()


def finish(fin, table, loss_out, ug_out, ig_out):
    clients, clusters = loss_out.shape
    ug_out[0] = fin[0]
    ig_out[0] = fin[1]
    loss_out[...] = table[...].reshape(clusters, 128).T[:clients, :]


def body(user_feats, item_feats, item_ids, picks, user_weight, item_weight):
    clients = picks.shape[0]
    total, depth = user_feats.shape
    rows = total // clients
    width = user_weight.shape[2]
    clusters = lax.axis_size("cluster")
    groups = 4
    grp = total // groups
    split = 56
    rest = 128 - split
    vmem = pltpu.VMEM
    dma = pltpu.SemaphoreType.DMA
    hbm_spec = pl.BlockSpec(memory_space=pltpu.HBM)
    vmem_spec = pl.BlockSpec(memory_space=pltpu.VMEM)
    uf, itf, ids, picks, uw, iw = [pltpu.with_memory_space_constraint(a, pltpu.HBM) for a in (
        user_feats, item_feats, item_ids.reshape(total // 128, 128), picks, user_weight, item_weight)]
    us, its, cu, ci = pl.pallas_call(
        functools.partial(picked, (clients, rows, width)),
        out_shape=tuple(jax.ShapeDtypeStruct((total, n), BF16) for n in (width, width, 256, 256)),
        in_specs=[hbm_spec] * 6,
        out_specs=(vmem_spec,) * 4,
        scratch_shapes=[
            vmem((total // 128, 128), jnp.int32), pltpu.SMEM((clients,), jnp.int32), pltpu.SMEM((clients,), jnp.int32),
            vmem((depth, width), BF16), vmem((depth, width), BF16),
            vmem((2, PAIR * rows, depth), BF16), vmem((2, PAIR * rows, depth), BF16),
            vmem((PAIR * rows, width), F32), vmem((PAIR * rows, width), BF16), vmem((PAIR * rows, width), BF16),
            dma((6,)), dma((2, 2, PAIR)),
        ],
        compiler_params=pltpu.CompilerParams(vmem_limit_bytes=PICKED_BYTES),
        name="picked",
    )(uf, itf, ids, picks, uw, iw)
    fin, table = pl.pallas_call(
        functools.partial(kernel, (clients, rows, width, split, groups, clusters)),
        out_shape=(jax.ShapeDtypeStruct((2, 128, width), F32), jax.ShapeDtypeStruct((2, clusters // 2, 1, 128), F32)),
        in_specs=[hbm_spec] * 5 + [vmem_spec] * 4,
        out_specs=(vmem_spec, vmem_spec),
        scratch_shapes=[
            vmem((total // 128, 128), jnp.int32),
            vmem((total, depth), BF16), vmem((total, depth), BF16),
            vmem((depth, width), BF16), vmem((depth, width), BF16),
            vmem((grp, width), BF16), vmem((grp, width), BF16),
            vmem((8, 2, 2, 128, width), F32), vmem((8, 2, 128, width), F32),
            vmem((4, 2, split, width), F32), vmem((2, rest, width), F32),
            vmem((2, split, width), F32), vmem((2, split, width), F32), vmem((2, split, width), F32),
            vmem((2, 2, rest, width), F32), vmem((2, 2, rest, width), F32), vmem((2, 2, rest, width), F32),
            dma((2 * NX + 1, 3)), dma((8, 2)), dma((8, 2)), dma((5, 2)), dma((5, 2)),
            dma((3, 3, 2)), dma((3, 3, 2)), dma((clusters,)), dma((clusters,)),
        ],
        compiler_params=pltpu.CompilerParams(
            collective_id=0, has_side_effects=True, vmem_limit_bytes=ROUND_BYTES),
        name="round",
    )(uf, itf, ids, uw, iw, us, its, cu, ci)
    return pl.pallas_call(
        finish,
        out_shape=(
            jax.ShapeDtypeStruct((clients, clusters), F32),
            jax.ShapeDtypeStruct((1, depth // 16, width), F32),
            jax.ShapeDtypeStruct((1, depth // 16, width), F32),
        ),
        in_specs=[vmem_spec, vmem_spec],
        out_specs=(vmem_spec, vmem_spec, vmem_spec),
        compiler_params=pltpu.CompilerParams(vmem_limit_bytes=FINISH_BYTES),
        name="finish",
    )(fin, table)


def solution(mesh):
    in_specs = (P("client", None), P("client", None), P("client"), P("client"),
                P("cluster", None, None), P("cluster", None, None))
    out_specs = (P("client", None), P("cluster", "client", None), P("cluster", "client", None))
    return jax.shard_map(body, mesh=mesh, in_specs=in_specs, out_specs=out_specs, check_vma=False)
```

```python
import functools
import math

import jax
import jax.numpy as jnp
from jax import lax
from jax.experimental import pallas as pl
from jax.experimental.pallas import tpu as pltpu
from jax.sharding import PartitionSpec as P

MESH = pl.DeviceIdType.MESH
NX = 4
ORDER = (2, 1, 3, 0)
PAIR = 2
PICKED_BYTES = 24 * 1024 * 1024
ROUND_BYTES = 46 * 1024 * 1024
FINISH_BYTES = 8 * 1024 * 1024
F32, BF16 = jnp.float32, jnp.bfloat16


def dot(a, b, dims=((1,), (0,))):
    return lax.dot_general(a, b, (dims, ((), ())), preferred_element_type=F32)


def same_item(ids, first, off, rows):
    shape = (rows, 128)
    last = ids.shape[0] - 1
    back = (128 - off) % 128
    got = pltpu.roll(jnp.broadcast_to(ids[pl.ds(first, 1), :], shape), back, 1)
    more = pltpu.roll(jnp.broadcast_to(ids[pl.ds(jnp.minimum(first + 1, last), 1), :], shape), back, 1)
    got = jnp.where(lax.broadcasted_iota(jnp.int32, shape, 1) < 128 - off, got, more)[:, :rows]
    return got == got.T


def columns(s_me, step):
    q = step // 2
    dx = (2 + 3 * q + 3 * (q * (q - 1) // 2)) % NX
    dy = 1 - step % 2
    chip = ((s_me // 4 + dx) % NX) * 2 + ((s_me // 2) % 2 + dy) % 2
    return pl.ds(pl.multiple_of(chip * 256, 256), 256)


def picked(cfg, uf, itf, ids_hbm, picks_hbm, uw, iw, us_out, is_out, cu_out, ci_out,
           ids, picks, chosen, wu, wi, bu, bi, dsilu, uvec, iv, sem, bsem):
    clients, rows, width = cfg
    temper = 1.0 / math.sqrt(width)
    k_me = lax.axis_index("cluster")
    loads = [pltpu.make_async_copy(src, dst, sem.at[n]) for n, (src, dst) in enumerate(
        ((picks_hbm, picks), (uw.at[0], wu), (iw.at[0], wi), (ids_hbm, ids)))]
    for copy in loads:
        copy.start()
    loads[0].wait()

    def scan(client, count):
        chosen[count] = client
        return count + jnp.where(picks[client] == k_me, 1, 0)

    count = lax.fori_loop(0, clients, scan, 0)

    @pl.when(count % PAIR == 1)
    def _():
        chosen[count] = chosen[count - 1]

    pairs = (count + 1) // PAIR

    def fetch(p):
        slot = p % 2
        copies = []
        for n in range(PAIR):
            at = pl.ds(pl.multiple_of(chosen[PAIR * p + n] * rows, rows), rows)
            to = pl.ds(n * rows, rows)
            copies.append(pltpu.make_async_copy(uf.at[at], bu.at[slot, to], bsem.at[slot, 0, n]))
            copies.append(pltpu.make_async_copy(itf.at[at], bi.at[slot, to], bsem.at[slot, 1, n]))
        return copies

    @pl.when(pairs > 0)
    def _():
        for copy in fetch(0):
            copy.start()

    def clear(n, carry):
        at = pl.ds(pl.multiple_of(n * 64, 64), 64)
        us_out[at, :] = jnp.zeros((64, width), BF16)
        is_out[at, :] = jnp.zeros((64, width), BF16)
        return carry

    first = columns(lax.axis_index("client"), 0)
    ahead = [pltpu.make_async_copy(src.at[:, first], dst, sem.at[4 + t])
             for t, (src, dst) in enumerate(((uf, cu_out), (itf, ci_out)))]
    for copy in ahead:
        copy.start()
    lax.fori_loop(0, clients * rows // 64, clear, 0)
    for copy in loads[1:]:
        copy.wait()

    def pair(p, carry):
        slot = p % 2

        @pl.when(p + 1 < pairs)
        def _():
            for copy in fetch(p + 1):
                copy.start()

        for copy in fetch(p):
            copy.wait()
        pre = dot(bu[slot], wu[...])
        sig = 0.5 * jnp.tanh(0.5 * pre) + 0.5
        u = pre * sig
        uvec[...] = u.astype(BF16)
        dsilu[...] = sig + (u - u * sig)
        iv[...] = dot(bi[slot], wi[...]).astype(BF16)
        for n in range(PAIR):
            client = chosen[PAIR * p + n]
            at = slice(n * rows, (n + 1) * rows)
            u = uvec[at, :]
            v = iv[at, :]
            s = dot(u, v, ((1,), (1,))) * temper
            start = client * rows
            same = same_item(ids, start // 128, start % 128, rows)
            gate = 0.5 * jnp.tanh(0.5 * s) + 0.5
            slope = (jnp.where(same, gate - 1.0, gate) * temper).astype(BF16)
            to = pl.ds(pl.multiple_of(start, rows), rows)
            us_out[to, :] = (dot(slope, v) * dsilu[at, :]).astype(BF16)
            is_out[to, :] = dot(slope, u, ((0,), (0,))).astype(BF16)
        return carry

    lax.fori_loop(0, pairs, pair, 0)
    for copy in ahead:
        copy.wait()


def kernel(cfg, uf, itf, ids_hbm, uw, iw, us, its, cu, ci, fin, table,
           ids, fu, fi, wu, wi, iv, uvec, gt, crecv, ya, yb,
           xa1, xal, xar, xb1, xbl, xbr,
           ld, cs, cr, ys, yr, xs, xr, ls, lr, up, down):
    clients, rows, width, split, groups, clusters = cfg
    total, depth = fu.shape
    per = clients // groups
    grp = per * rows
    temper = 1.0 / math.sqrt(width)
    k_me = lax.axis_index("cluster")
    s_me = lax.axis_index("client")
    x = s_me // 4
    y = (s_me // 2) % 2
    c = s_me % 2
    mate = {"client": x * 4 + y * 2 + (1 - c)}
    across = {"client": x * 4 + (1 - y) * 2 + c}
    right = {"client": ((x + 1) % NX) * 4 + y * 2 + c}
    left = {"client": ((x + NX - 1) % NX) * 4 + y * 2 + c}
    nz = clusters // 2
    h = k_me // nz
    z = k_me % nz
    twin = {"cluster": (1 - h) * nz + z}
    above = {"cluster": h * nz + (z + 1) % nz}
    below = {"cluster": h * nz + (z + nz - 1) % nz}

    barrier = pltpu.get_barrier_semaphore()
    for peer in (mate, across, right, left, twin, above, below):
        pl.semaphore_signal(barrier, inc=1, device_id=peer, device_id_type=MESH)

    def feats(step, t):
        src, dst = ((uf, fu), (itf, fi))[t]
        at = columns(s_me, step)
        return pltpu.make_async_copy(src.at[:, at], dst.at[:, at], ld.at[step, t])

    rest_loads = [pltpu.make_async_copy(src, dst, ld.at[2 * NX, n]) for n, (src, dst) in enumerate(
        ((uw.at[0], wu), (iw.at[0], wi), (ids_hbm, ids)))]
    for step in (1, 2):
        for t in (0, 1):
            feats(step, t).start()

    A = pl.ds(0, split)
    B = pl.ds(split, 128 - split)

    def step_of(dx, dy):
        return 2 * ORDER.index(dx) + (1 - dy)

    def own(dx, dy, t, part):
        return gt.at[step_of(dx, dy), t, c, part]

    def send(src, dst, ssem, rsem, peer):
        return pltpu.make_async_remote_copy(src_ref=src, dst_ref=dst, send_sem=ssem, recv_sem=rsem,
                                            device_id=peer, device_id_type=MESH)

    def tell(n):
        if n > 1:
            pl.semaphore_wait(up.at[n - 1], 1)
            if n <= nz // 2:
                pl.semaphore_wait(down.at[n - 1], 1)
        if n <= nz // 2:
            pl.semaphore_signal(up.at[n], inc=1, device_id=above, device_id_type=MESH)
        if n < nz // 2:
            pl.semaphore_signal(down.at[n], inc=1, device_id=below, device_id_type=MESH)

    def loss_copy(n):
        mine = table.at[h, z]
        return send(mine, mine, ls.at[n], lr.at[n], {"cluster": (k_me + n) % clusters})

    def core_copy(step, t):
        return send(gt.at[step, t, 1 - c], crecv.at[step, t], cs.at[step, t], cr.at[step, t], mate)

    def ya_copy(dx, t):
        return send(own(dx, 1, t, A), ya.at[dx, t], ys.at[dx, t], yr.at[dx, t], across)

    def yb_copy(t):
        return send(own(0, 1, t, B), yb.at[t], ys.at[4, t], yr.at[4, t], across)

    def x_part(which):
        return (0, A, xa1, xal, xar) if which == 2 else (which, B, xb1.at[which], xbl.at[which], xbr.at[which])

    def far_copy(which, t):
        dy, part, first, _, _ = x_part(which)
        return send(own(2, dy, t, part), first.at[t], xs.at[which, 0, t], xr.at[which, 0, t], (right, left)[t])

    def near_copy(which, t, rightward):
        dy, part, _, from_left, from_right = x_part(which)
        if rightward:
            return send(own(1, dy, t, part), from_left.at[t], xs.at[which, 1, t], xr.at[which, 1, t], right)
        return send(own(3, dy, t, part), from_right.at[t], xs.at[which, 2, t], xr.at[which, 2, t], left)

    def add(dst, src):
        dst[...] += src[...]

    def far_arrived(which, t):
        dy, part, first, _, _ = x_part(which)
        far_copy(which, t).wait_recv()
        add(own((1, 3)[t], dy, t, part), first.at[t])
        near_copy(which, t, t == 0).start()

    def near_arrived(which):
        dy, part, _, from_left, from_right = x_part(which)
        for t in (0, 1):
            near_copy(which, t, True).wait_recv()
            near_copy(which, t, False).wait_recv()
            mine = own(0, dy, t, part)
            mine[...] += from_left[t] + from_right[t]

    def ya_arrived(dx):
        for t in (0, 1):
            ya_copy(dx, t).wait_recv()
            add(own(dx, 0, t, A), ya.at[dx, t])

    def ready(step):
        dx, dy = ORDER[step // 2], 1 - step % 2
        for t in (0, 1):
            core_copy(step, t).wait_recv()
            mine = gt.at[step, t, c]
            mine[...] += crecv[step, t]
            if dx == 2:
                far_copy(dy, t).start()
            if dy == 1:
                ya_copy(dx, t).start()
            if dx == 1 and t == 1:
                near_copy(dy, 1, True).start()
            if dx == 3 and t == 0:
                near_copy(dy, 0, False).start()

    def block(step, lhs):
        for t, (slope, feat) in enumerate(((us, lhs[0]), (its, lhs[1]))):
            r = dot(feat(), slope[...], ((0,), (0,)))
            gt[step, t, 0] = r[:128]
            gt[step, t, 1] = r[128:]
            if isinstance(step, int) and step == 0 and t == 0:
                pl.semaphore_wait(barrier, 7)
                tell(1)
            core_copy(step, t).start()

    def loaded(step):
        def of(t, buf):
            feats(step, t).wait()
            return buf[:, columns(s_me, step)]
        return functools.partial(of, 0, fu), functools.partial(of, 1, fi)

    def blocks(step, carry):
        @pl.when(step + 2 < 2 * NX)
        def _():
            for t in (0, 1):
                feats(step + 2, t).start()

        @pl.when(step == 2 * NX - 3)
        def _():
            for copy in rest_loads:
                copy.start()
            for t in (0, 1):
                feats(0, t).start()

        block(step, loaded(step))
        for n in range(2 * NX - 2):
            @pl.when(step == n + 1)
            def _(n=n):
                ready(n)
                if n == 5:
                    far_arrived(1, 0)
                    far_arrived(1, 1)
        return carry

    block(0, (lambda: cu[...], lambda: ci[...]))
    lax.fori_loop(1, 2 * NX - 1, blocks, 0)
    ready(2 * NX - 2)
    far_arrived(0, 0)
    far_arrived(0, 1)
    for copy in rest_loads:
        copy.wait()
    for t in (0, 1):
        feats(0, t).wait()
        feats(2 * NX - 1, t).wait()

    lane = lax.broadcasted_iota(jnp.int32, (1, 128), 1)

    def losses_of(g, losses):
        at = pl.ds(pl.multiple_of(g * grp, grp), grp)
        pre = dot(fu[at, :], wu[...])
        uvec[...] = (pre * (0.5 * jnp.tanh(0.5 * pre) + 0.5)).astype(BF16)
        iv[...] = dot(fi[at, :], wi[...]).astype(BF16)
        for n in range(per):
            rows_n = slice(n * rows, (n + 1) * rows)
            s = dot(uvec[rows_n, :], iv[rows_n, :], ((1,), (1,))) * temper
            first, off = divmod(n * rows, 128)
            same = same_item(ids, g * (grp // 128) + first, off, rows)
            pair = jnp.maximum(s, 0.0) + jnp.log(1.0 + jnp.exp(-jnp.abs(s))) - jnp.where(same, s, 0.0)
            mean = jnp.sum(pair, axis=(0, 1), keepdims=True) * (1.0 / (rows * rows))
            losses = jnp.where(lane == g * per + n, mean, losses)

        for m in range(groups):
            @pl.when(g == m)
            def _(m=m):
                tell(m + 2)

        @pl.when(g == 0)
        def _():
            ya_arrived(2)
            far_copy(2, 0).start()
            far_copy(2, 1).start()

        @pl.when(g == 1)
        def _():
            ya_arrived(1)
            near_copy(2, 1, True).start()

        return losses

    losses = lax.fori_loop(0, groups, losses_of, jnp.zeros((1, 128), F32))
    table[h, z] = losses
    for n in range(1, clusters):
        loss_copy(n).start()
    block(2 * NX - 1, (lambda: fu[:, columns(s_me, 2 * NX - 1)], lambda: fi[:, columns(s_me, 2 * NX - 1)]))
    ya_arrived(3)
    near_copy(2, 0, False).start()
    near_arrived(1)
    yb_copy(0).start()
    yb_copy(1).start()
    ready(2 * NX - 1)
    far_arrived(2, 0)
    far_arrived(2, 1)
    near_arrived(0)
    ya_arrived(0)
    for t in (0, 1):
        yb_copy(t).wait_recv()
        fin[t, split:, :] = gt[step_of(0, 0), t, c, split:, :] + yb[t]
    for t in (0, 1):
        near_copy(2, t, True).wait_recv()
        near_copy(2, t, False).wait_recv()
        fin[t, :split, :] = gt[step_of(0, 0), t, c, :split, :] + xal[t] + xar[t]

    for n in range(1, clusters):
        loss_copy(n).wait()
    for step in range(2 * NX):
        for t in (0, 1):
            core_copy(step, t).wait_send()
    for t in (0, 1):
        for dx in range(NX):
            ya_copy(dx, t).wait_send()
        yb_copy(t).wait_send()
        for which in range(3):
            far_copy(which, t).wait_send()
            near_copy(which, t, True).wait_send()
            near_copy(which, t, False).wait_send()


def finish(fin, table, loss_out, ug_out, ig_out):
    clients, clusters = loss_out.shape
    ug_out[0] = fin[0]
    ig_out[0] = fin[1]
    loss_out[...] = table[...].reshape(clusters, 128).T[:clients, :]


def body(user_feats, item_feats, item_ids, picks, user_weight, item_weight):
    clients = picks.shape[0]
    total, depth = user_feats.shape
    rows = total // clients
    width = user_weight.shape[2]
    clusters = lax.axis_size("cluster")
    groups = 4
    grp = total // groups
    split = 56
    rest = 128 - split
    vmem = pltpu.VMEM
    dma = pltpu.SemaphoreType.DMA
    hbm_spec = pl.BlockSpec(memory_space=pltpu.HBM)
    vmem_spec = pl.BlockSpec(memory_space=pltpu.VMEM)
    uf, itf, ids, picks, uw, iw = [pltpu.with_memory_space_constraint(a, pltpu.HBM) for a in (
        user_feats, item_feats, item_ids.reshape(total // 128, 128), picks, user_weight, item_weight)]
    us, its, cu, ci = pl.pallas_call(
        functools.partial(picked, (clients, rows, width)),
        out_shape=tuple(jax.ShapeDtypeStruct((total, n), BF16) for n in (width, width, 256, 256)),
        in_specs=[hbm_spec] * 6,
        out_specs=(vmem_spec,) * 4,
        scratch_shapes=[
            vmem((total // 128, 128), jnp.int32), pltpu.SMEM((clients,), jnp.int32), pltpu.SMEM((clients,), jnp.int32),
            vmem((depth, width), BF16), vmem((depth, width), BF16),
            vmem((2, PAIR * rows, depth), BF16), vmem((2, PAIR * rows, depth), BF16),
            vmem((PAIR * rows, width), F32), vmem((PAIR * rows, width), BF16), vmem((PAIR * rows, width), BF16),
            dma((6,)), dma((2, 2, PAIR)),
        ],
        compiler_params=pltpu.CompilerParams(vmem_limit_bytes=PICKED_BYTES),
        name="picked",
    )(uf, itf, ids, picks, uw, iw)
    fin, table = pl.pallas_call(
        functools.partial(kernel, (clients, rows, width, split, groups, clusters)),
        out_shape=(jax.ShapeDtypeStruct((2, 128, width), F32), jax.ShapeDtypeStruct((2, clusters // 2, 1, 128), F32)),
        in_specs=[hbm_spec] * 5 + [vmem_spec] * 4,
        out_specs=(vmem_spec, vmem_spec),
        scratch_shapes=[
            vmem((total // 128, 128), jnp.int32),
            vmem((total, depth), BF16), vmem((total, depth), BF16),
            vmem((depth, width), BF16), vmem((depth, width), BF16),
            vmem((grp, width), BF16), vmem((grp, width), BF16),
            vmem((8, 2, 2, 128, width), F32), vmem((8, 2, 128, width), F32),
            vmem((4, 2, split, width), F32), vmem((2, rest, width), F32),
            vmem((2, split, width), F32), vmem((2, split, width), F32), vmem((2, split, width), F32),
            vmem((2, 2, rest, width), F32), vmem((2, 2, rest, width), F32), vmem((2, 2, rest, width), F32),
            dma((2 * NX + 1, 3)), dma((8, 2)), dma((8, 2)), dma((5, 2)), dma((5, 2)),
            dma((3, 3, 2)), dma((3, 3, 2)), dma((clusters,)), dma((clusters,)),
            pltpu.SemaphoreType.REGULAR((5,)), pltpu.SemaphoreType.REGULAR((5,)),
        ],
        compiler_params=pltpu.CompilerParams(
            collective_id=0, has_side_effects=True, vmem_limit_bytes=ROUND_BYTES),
        name="round",
    )(uf, itf, ids, uw, iw, us, its, cu, ci)
    return pl.pallas_call(
        finish,
        out_shape=(
            jax.ShapeDtypeStruct((clients, clusters), F32),
            jax.ShapeDtypeStruct((1, depth // 16, width), F32),
            jax.ShapeDtypeStruct((1, depth // 16, width), F32),
        ),
        in_specs=[vmem_spec, vmem_spec],
        out_specs=(vmem_spec, vmem_spec, vmem_spec),
        compiler_params=pltpu.CompilerParams(vmem_limit_bytes=FINISH_BYTES),
        name="finish",
    )(fin, table)


def solution(mesh):
    in_specs = (P("client", None), P("client", None), P("client"), P("client"),
                P("cluster", None, None), P("cluster", None, None))
    out_specs = (P("client", None), P("cluster", "client", None), P("cluster", "client", None))
    return jax.shard_map(body, mesh=mesh, in_specs=in_specs, out_specs=out_specs, check_vma=False)
```

```python
import functools
import math

import jax
import jax.numpy as jnp
from jax import lax
from jax.experimental import pallas as pl
from jax.experimental.pallas import tpu as pltpu
from jax.sharding import PartitionSpec as P

MESH = pl.DeviceIdType.MESH
NX = 4
ORDER = (2, 1, 3, 0)
PAIR = 2
PICKED_BYTES = 24 * 1024 * 1024
ROUND_BYTES = 46 * 1024 * 1024
FINISH_BYTES = 8 * 1024 * 1024
F32, BF16 = jnp.float32, jnp.bfloat16


def dot(a, b, dims=((1,), (0,))):
    return lax.dot_general(a, b, (dims, ((), ())), preferred_element_type=F32)


def same_item(ids, first, off, rows):
    shape = (rows, 128)
    last = ids.shape[0] - 1
    back = (128 - off) % 128
    got = pltpu.roll(jnp.broadcast_to(ids[pl.ds(first, 1), :], shape), back, 1)
    more = pltpu.roll(jnp.broadcast_to(ids[pl.ds(jnp.minimum(first + 1, last), 1), :], shape), back, 1)
    got = jnp.where(lax.broadcasted_iota(jnp.int32, shape, 1) < 128 - off, got, more)[:, :rows]
    return got == got.T


def columns(s_me, step):
    q = step // 2
    dx = (2 + 3 * q + 3 * (q * (q - 1) // 2)) % NX
    dy = 1 - step % 2
    chip = ((s_me // 4 + dx) % NX) * 2 + ((s_me // 2) % 2 + dy) % 2
    return pl.ds(pl.multiple_of(chip * 256, 256), 256)


def picked(cfg, uf, itf, ids_hbm, picks_hbm, uw, iw, us_out, is_out, cu_out, ci_out,
           ids, picks, chosen, wu, wi, bu, bi, dsilu, uvec, iv, sem, bsem):
    clients, rows, width = cfg
    temper = 1.0 / math.sqrt(width)
    k_me = lax.axis_index("cluster")
    loads = [pltpu.make_async_copy(src, dst, sem.at[n]) for n, (src, dst) in enumerate(
        ((picks_hbm, picks), (uw.at[0], wu), (iw.at[0], wi), (ids_hbm, ids)))]
    for copy in loads:
        copy.start()
    loads[0].wait()

    def scan(client, count):
        chosen[count] = client
        return count + jnp.where(picks[client] == k_me, 1, 0)

    count = lax.fori_loop(0, clients, scan, 0)

    @pl.when(count % PAIR == 1)
    def _():
        chosen[count] = chosen[count - 1]

    pairs = (count + 1) // PAIR

    def fetch(p):
        slot = p % 2
        copies = []
        for n in range(PAIR):
            at = pl.ds(pl.multiple_of(chosen[PAIR * p + n] * rows, rows), rows)
            to = pl.ds(n * rows, rows)
            copies.append(pltpu.make_async_copy(uf.at[at], bu.at[slot, to], bsem.at[slot, 0, n]))
            copies.append(pltpu.make_async_copy(itf.at[at], bi.at[slot, to], bsem.at[slot, 1, n]))
        return copies

    @pl.when(pairs > 0)
    def _():
        for copy in fetch(0):
            copy.start()

    def clear(n, carry):
        at = pl.ds(pl.multiple_of(n * 64, 64), 64)
        us_out[at, :] = jnp.zeros((64, width), BF16)
        is_out[at, :] = jnp.zeros((64, width), BF16)
        return carry

    first = columns(lax.axis_index("client"), 0)
    ahead = [pltpu.make_async_copy(src.at[:, first], dst, sem.at[4 + t])
             for t, (src, dst) in enumerate(((uf, cu_out), (itf, ci_out)))]
    for copy in ahead:
        copy.start()
    lax.fori_loop(0, clients * rows // 64, clear, 0)
    for copy in loads[1:]:
        copy.wait()

    def pair(p, carry):
        slot = p % 2

        @pl.when(p + 1 < pairs)
        def _():
            for copy in fetch(p + 1):
                copy.start()

        for copy in fetch(p):
            copy.wait()
        pre = dot(bu[slot], wu[...])
        sig = 0.5 * jnp.tanh(0.5 * pre) + 0.5
        u = pre * sig
        uvec[...] = u.astype(BF16)
        dsilu[...] = sig + (u - u * sig)
        iv[...] = dot(bi[slot], wi[...]).astype(BF16)
        for n in range(PAIR):
            client = chosen[PAIR * p + n]
            at = slice(n * rows, (n + 1) * rows)
            u = uvec[at, :]
            v = iv[at, :]
            s = dot(u, v, ((1,), (1,))) * temper
            start = client * rows
            same = same_item(ids, start // 128, start % 128, rows)
            gate = 0.5 * jnp.tanh(0.5 * s) + 0.5
            slope = (jnp.where(same, gate - 1.0, gate) * temper).astype(BF16)
            to = pl.ds(pl.multiple_of(start, rows), rows)
            us_out[to, :] = (dot(slope, v) * dsilu[at, :]).astype(BF16)
            is_out[to, :] = dot(slope, u, ((0,), (0,))).astype(BF16)
        return carry

    lax.fori_loop(0, pairs, pair, 0)
    for copy in ahead:
        copy.wait()


def kernel(cfg, uf, itf, ids_hbm, uw, iw, us, its, cu, ci, fin, table,
           ids, fu, fi, wu, wi, iv, uvec, gt, crecv, ya, yb,
           xa1, xal, xar, xb1, xbl, xbr,
           ld, cs, cr, ys, yr, xs, xr, ls, lr, up, down):
    clients, rows, width, split, groups, clusters = cfg
    total, depth = fu.shape
    per = clients // groups
    grp = per * rows
    temper = 1.0 / math.sqrt(width)
    k_me = lax.axis_index("cluster")
    s_me = lax.axis_index("client")
    x = s_me // 4
    y = (s_me // 2) % 2
    c = s_me % 2
    mate = {"client": x * 4 + y * 2 + (1 - c)}
    across = {"client": x * 4 + (1 - y) * 2 + c}
    right = {"client": ((x + 1) % NX) * 4 + y * 2 + c}
    left = {"client": ((x + NX - 1) % NX) * 4 + y * 2 + c}
    nz = clusters // 2
    h = k_me // nz
    z = k_me % nz
    twin = {"cluster": (1 - h) * nz + z}
    above = {"cluster": h * nz + (z + 1) % nz}
    below = {"cluster": h * nz + (z + nz - 1) % nz}
    has_above = z < nz - 1
    has_below = z > 0

    barrier = pltpu.get_barrier_semaphore()
    for peer in (mate, across, right, left, twin):
        pl.semaphore_signal(barrier, inc=1, device_id=peer, device_id_type=MESH)
    for there, peer in ((has_above, above), (has_below, below)):
        @pl.when(there)
        def _(peer=peer):
            pl.semaphore_signal(barrier, inc=1, device_id=peer, device_id_type=MESH)

    def feats(step, t):
        src, dst = ((uf, fu), (itf, fi))[t]
        at = columns(s_me, step)
        return pltpu.make_async_copy(src.at[:, at], dst.at[:, at], ld.at[step, t])

    rest_loads = [pltpu.make_async_copy(src, dst, ld.at[2 * NX, n]) for n, (src, dst) in enumerate(
        ((uw.at[0], wu), (iw.at[0], wi), (ids_hbm, ids)))]
    for step in (1, 2):
        for t in (0, 1):
            feats(step, t).start()

    A = pl.ds(0, split)
    B = pl.ds(split, 128 - split)

    def step_of(dx, dy):
        return 2 * ORDER.index(dx) + (1 - dy)

    def own(dx, dy, t, part):
        return gt.at[step_of(dx, dy), t, c, part]

    def send(src, dst, ssem, rsem, peer):
        return pltpu.make_async_remote_copy(src_ref=src, dst_ref=dst, send_sem=ssem, recv_sem=rsem,
                                            device_id=peer, device_id_type=MESH)

    def pass_on(sem, has_source, has_target, target):
        @pl.when(has_source)
        def _():
            pl.semaphore_wait(sem, 1)

        @pl.when(has_target)
        def _():
            pl.semaphore_signal(sem, inc=1, device_id=target, device_id_type=MESH)

    def tell(n):
        @pl.when((z + 1) // 2 == n)
        def _():
            pass_on(up, has_below, has_above, above)

        @pl.when((nz - z) // 2 == n)
        def _():
            pass_on(down, has_above, has_below, below)

    def loss_copy(n):
        mine = table.at[h, z]
        return send(mine, mine, ls.at[n], lr.at[n], {"cluster": (k_me + n) % clusters})

    def core_copy(step, t):
        return send(gt.at[step, t, 1 - c], crecv.at[step, t], cs.at[step, t], cr.at[step, t], mate)

    def ya_copy(dx, t):
        return send(own(dx, 1, t, A), ya.at[dx, t], ys.at[dx, t], yr.at[dx, t], across)

    def yb_copy(t):
        return send(own(0, 1, t, B), yb.at[t], ys.at[4, t], yr.at[4, t], across)

    def x_part(which):
        return (0, A, xa1, xal, xar) if which == 2 else (which, B, xb1.at[which], xbl.at[which], xbr.at[which])

    def far_copy(which, t):
        dy, part, first, _, _ = x_part(which)
        return send(own(2, dy, t, part), first.at[t], xs.at[which, 0, t], xr.at[which, 0, t], (right, left)[t])

    def near_copy(which, t, rightward):
        dy, part, _, from_left, from_right = x_part(which)
        if rightward:
            return send(own(1, dy, t, part), from_left.at[t], xs.at[which, 1, t], xr.at[which, 1, t], right)
        return send(own(3, dy, t, part), from_right.at[t], xs.at[which, 2, t], xr.at[which, 2, t], left)

    def add(dst, src):
        dst[...] += src[...]

    def far_arrived(which, t):
        dy, part, first, _, _ = x_part(which)
        far_copy(which, t).wait_recv()
        add(own((1, 3)[t], dy, t, part), first.at[t])
        near_copy(which, t, t == 0).start()

    def near_arrived(which):
        dy, part, _, from_left, from_right = x_part(which)
        for t in (0, 1):
            near_copy(which, t, True).wait_recv()
            near_copy(which, t, False).wait_recv()
            mine = own(0, dy, t, part)
            mine[...] += from_left[t] + from_right[t]

    def ya_arrived(dx):
        for t in (0, 1):
            ya_copy(dx, t).wait_recv()
            add(own(dx, 0, t, A), ya.at[dx, t])

    def ready(step, t):
        dx, dy = ORDER[step // 2], 1 - step % 2
        core_copy(step, t).wait_recv()
        mine = gt.at[step, t, c]
        mine[...] += crecv[step, t]
        if dx == 2:
            far_copy(dy, t).start()
        if dy == 1:
            ya_copy(dx, t).start()
        if dx == 1 and t == 1:
            near_copy(dy, 1, True).start()
        if dx == 3 and t == 0:
            near_copy(dy, 0, False).start()

    def block(step, lhs):
        for t, (slope, feat) in enumerate(((us, lhs[0]), (its, lhs[1]))):
            r = dot(feat(), slope[...], ((0,), (0,)))
            gt[step, t, 0] = r[:128]
            gt[step, t, 1] = r[128:]
            if isinstance(step, int) and step == 0 and t == 0:
                ends = (z + nz - 2) // (nz - 1) + (2 * nz - 3 - z) // (nz - 1)
                pl.semaphore_wait(barrier, 5 + ends)
                tell(0)
            core_copy(step, t).start()
            for n in range(2 * NX - 2):
                if not isinstance(step, int):
                    @pl.when(step == n + 1)
                    def _(n=n, t=t):
                        ready(n, t)

    def loaded(step):
        def of(t, buf):
            feats(step, t).wait()
            return buf[:, columns(s_me, step)]
        return functools.partial(of, 0, fu), functools.partial(of, 1, fi)

    def blocks(step, carry):
        @pl.when(step + 2 < 2 * NX)
        def _():
            for t in (0, 1):
                feats(step + 2, t).start()

        @pl.when(step == 2 * NX - 3)
        def _():
            for copy in rest_loads:
                copy.start()
            for t in (0, 1):
                feats(0, t).start()

        block(step, loaded(step))
        @pl.when(step == 2 * NX - 2)
        def _():
            far_arrived(1, 0)
            far_arrived(1, 1)

        return carry

    block(0, (lambda: cu[...], lambda: ci[...]))
    lax.fori_loop(1, 2 * NX - 1, blocks, 0)
    ready(2 * NX - 2, 0)
    ready(2 * NX - 2, 1)
    far_arrived(0, 0)
    far_arrived(0, 1)
    for copy in rest_loads:
        copy.wait()
    for t in (0, 1):
        feats(0, t).wait()
        feats(2 * NX - 1, t).wait()

    lane = lax.broadcasted_iota(jnp.int32, (1, 128), 1)

    def losses_of(g, losses):
        at = pl.ds(pl.multiple_of(g * grp, grp), grp)
        pre = dot(fu[at, :], wu[...])
        uvec[...] = (pre * (0.5 * jnp.tanh(0.5 * pre) + 0.5)).astype(BF16)
        iv[...] = dot(fi[at, :], wi[...]).astype(BF16)
        for n in range(per):
            rows_n = slice(n * rows, (n + 1) * rows)
            s = dot(uvec[rows_n, :], iv[rows_n, :], ((1,), (1,))) * temper
            first, off = divmod(n * rows, 128)
            same = same_item(ids, g * (grp // 128) + first, off, rows)
            pair = jnp.maximum(s, 0.0) + jnp.log(1.0 + jnp.exp(-jnp.abs(s))) - jnp.where(same, s, 0.0)
            mean = jnp.sum(pair, axis=(0, 1), keepdims=True) * (1.0 / (rows * rows))
            losses = jnp.where(lane == g * per + n, mean, losses)

        for m in range(groups):
            @pl.when(g == m)
            def _(m=m):
                tell(m + 1)

        @pl.when(g == 0)
        def _():
            ya_arrived(2)
            far_copy(2, 0).start()
            far_copy(2, 1).start()

        @pl.when(g == 1)
        def _():
            ya_arrived(1)
            near_copy(2, 1, True).start()

        return losses

    losses = lax.fori_loop(0, groups, losses_of, jnp.zeros((1, 128), F32))
    table[h, z] = losses
    for n in range(1, clusters):
        loss_copy(n).start()
    block(2 * NX - 1, (lambda: fu[:, columns(s_me, 2 * NX - 1)], lambda: fi[:, columns(s_me, 2 * NX - 1)]))
    ya_arrived(3)
    near_copy(2, 0, False).start()
    near_arrived(1)
    yb_copy(0).start()
    yb_copy(1).start()
    ready(2 * NX - 1, 0)
    ready(2 * NX - 1, 1)
    far_arrived(2, 0)
    far_arrived(2, 1)
    near_arrived(0)
    ya_arrived(0)
    for t in (0, 1):
        yb_copy(t).wait_recv()
        fin[t, split:, :] = gt[step_of(0, 0), t, c, split:, :] + yb[t]
    for t in (0, 1):
        near_copy(2, t, True).wait_recv()
        near_copy(2, t, False).wait_recv()
        fin[t, :split, :] = gt[step_of(0, 0), t, c, :split, :] + xal[t] + xar[t]

    for n in range(1, clusters):
        loss_copy(n).wait()
    for step in range(2 * NX):
        for t in (0, 1):
            core_copy(step, t).wait_send()
    for t in (0, 1):
        for dx in range(NX):
            ya_copy(dx, t).wait_send()
        yb_copy(t).wait_send()
        for which in range(3):
            far_copy(which, t).wait_send()
            near_copy(which, t, True).wait_send()
            near_copy(which, t, False).wait_send()


def finish(fin, table, loss_out, ug_out, ig_out):
    clients, clusters = loss_out.shape
    ug_out[0] = fin[0]
    ig_out[0] = fin[1]
    loss_out[...] = table[...].reshape(clusters, 128).T[:clients, :]


def body(user_feats, item_feats, item_ids, picks, user_weight, item_weight):
    clients = picks.shape[0]
    total, depth = user_feats.shape
    rows = total // clients
    width = user_weight.shape[2]
    clusters = lax.axis_size("cluster")
    groups = 4
    grp = total // groups
    split = 56
    rest = 128 - split
    vmem = pltpu.VMEM
    dma = pltpu.SemaphoreType.DMA
    hbm_spec = pl.BlockSpec(memory_space=pltpu.HBM)
    vmem_spec = pl.BlockSpec(memory_space=pltpu.VMEM)
    uf, itf, ids, picks, uw, iw = [pltpu.with_memory_space_constraint(a, pltpu.HBM) for a in (
        user_feats, item_feats, item_ids.reshape(total // 128, 128), picks, user_weight, item_weight)]
    us, its, cu, ci = pl.pallas_call(
        functools.partial(picked, (clients, rows, width)),
        out_shape=tuple(jax.ShapeDtypeStruct((total, n), BF16) for n in (width, width, 256, 256)),
        in_specs=[hbm_spec] * 6,
        out_specs=(vmem_spec,) * 4,
        scratch_shapes=[
            vmem((total // 128, 128), jnp.int32), pltpu.SMEM((clients,), jnp.int32), pltpu.SMEM((clients,), jnp.int32),
            vmem((depth, width), BF16), vmem((depth, width), BF16),
            vmem((2, PAIR * rows, depth), BF16), vmem((2, PAIR * rows, depth), BF16),
            vmem((PAIR * rows, width), F32), vmem((PAIR * rows, width), BF16), vmem((PAIR * rows, width), BF16),
            dma((6,)), dma((2, 2, PAIR)),
        ],
        compiler_params=pltpu.CompilerParams(vmem_limit_bytes=PICKED_BYTES),
        name="picked",
    )(uf, itf, ids, picks, uw, iw)
    fin, table = pl.pallas_call(
        functools.partial(kernel, (clients, rows, width, split, groups, clusters)),
        out_shape=(jax.ShapeDtypeStruct((2, 128, width), F32), jax.ShapeDtypeStruct((2, clusters // 2, 1, 128), F32)),
        in_specs=[hbm_spec] * 5 + [vmem_spec] * 4,
        out_specs=(vmem_spec, vmem_spec),
        scratch_shapes=[
            vmem((total // 128, 128), jnp.int32),
            vmem((total, depth), BF16), vmem((total, depth), BF16),
            vmem((depth, width), BF16), vmem((depth, width), BF16),
            vmem((grp, width), BF16), vmem((grp, width), BF16),
            vmem((8, 2, 2, 128, width), F32), vmem((8, 2, 128, width), F32),
            vmem((4, 2, split, width), F32), vmem((2, rest, width), F32),
            vmem((2, split, width), F32), vmem((2, split, width), F32), vmem((2, split, width), F32),
            vmem((2, 2, rest, width), F32), vmem((2, 2, rest, width), F32), vmem((2, 2, rest, width), F32),
            dma((2 * NX + 1, 3)), dma((8, 2)), dma((8, 2)), dma((5, 2)), dma((5, 2)),
            dma((3, 3, 2)), dma((3, 3, 2)), dma((clusters,)), dma((clusters,)),
            pltpu.SemaphoreType.REGULAR, pltpu.SemaphoreType.REGULAR,
        ],
        compiler_params=pltpu.CompilerParams(
            collective_id=0, has_side_effects=True, vmem_limit_bytes=ROUND_BYTES),
        name="round",
    )(uf, itf, ids, uw, iw, us, its, cu, ci)
    return pl.pallas_call(
        finish,
        out_shape=(
            jax.ShapeDtypeStruct((clients, clusters), F32),
            jax.ShapeDtypeStruct((1, depth // 16, width), F32),
            jax.ShapeDtypeStruct((1, depth // 16, width), F32),
        ),
        in_specs=[vmem_spec, vmem_spec],
        out_specs=(vmem_spec, vmem_spec, vmem_spec),
        compiler_params=pltpu.CompilerParams(vmem_limit_bytes=FINISH_BYTES),
        name="finish",
    )(fin, table)


def solution(mesh):
    in_specs = (P("client", None), P("client", None), P("client"), P("client"),
                P("cluster", None, None), P("cluster", None, None))
    out_specs = (P("client", None), P("cluster", "client", None), P("cluster", "client", None))
    return jax.shard_map(body, mesh=mesh, in_specs=in_specs, out_specs=out_specs, check_vma=False)
```

```python
import functools
import math

import jax
import jax.numpy as jnp
from jax import lax
from jax.experimental import pallas as pl
from jax.experimental.pallas import tpu as pltpu
from jax.sharding import PartitionSpec as P

MESH = pl.DeviceIdType.MESH
NX = 4
STEPS = ((2, 1), (2, 0), (1, 1), (3, 1), (1, 0), (3, 0), (0, 1), (0, 0))
PAIR = 2
PICKED_BYTES = 24 * 1024 * 1024
ROUND_BYTES = 46 * 1024 * 1024
FINISH_BYTES = 8 * 1024 * 1024
F32, BF16 = jnp.float32, jnp.bfloat16


def dot(a, b, dims=((1,), (0,))):
    return lax.dot_general(a, b, (dims, ((), ())), preferred_element_type=F32)


def same_item(ids, first, off, rows):
    shape = (rows, 128)
    last = ids.shape[0] - 1
    back = (128 - off) % 128
    got = pltpu.roll(jnp.broadcast_to(ids[pl.ds(first, 1), :], shape), back, 1)
    more = pltpu.roll(jnp.broadcast_to(ids[pl.ds(jnp.minimum(first + 1, last), 1), :], shape), back, 1)
    got = jnp.where(lax.broadcasted_iota(jnp.int32, shape, 1) < 128 - off, got, more)[:, :rows]
    return got == got.T


def columns(s_me, step):
    q = (step + 2) // 4
    middle = q * (2 - q)
    dx = (1 - q) * (2 - q) + middle * (1 + 2 * (step % 2))
    dy = middle * (2 - step // 2) + (1 - middle) * (1 - step % 2)
    chip = ((s_me // 4 + dx) % NX) * 2 + ((s_me // 2) % 2 + dy) % 2
    return pl.ds(pl.multiple_of(chip * 256, 256), 256)


def picked(cfg, uf, itf, ids_hbm, picks_hbm, uw, iw, us_out, is_out, cu_out, ci_out,
           ids, picks, chosen, wu, wi, bu, bi, dsilu, uvec, iv, sem, bsem):
    clients, rows, width = cfg
    temper = 1.0 / math.sqrt(width)
    k_me = lax.axis_index("cluster")
    loads = [pltpu.make_async_copy(src, dst, sem.at[n]) for n, (src, dst) in enumerate(
        ((picks_hbm, picks), (uw.at[0], wu), (iw.at[0], wi), (ids_hbm, ids)))]
    for copy in loads[:2]:
        copy.start()
    loads[0].wait()

    def scan(client, count):
        chosen[count] = client
        return count + jnp.where(picks[client] == k_me, 1, 0)

    count = lax.fori_loop(0, clients, scan, 0)

    @pl.when(count % PAIR == 1)
    def _():
        chosen[count] = chosen[count - 1]

    pairs = (count + 1) // PAIR

    def fetch(p):
        slot = p % 2
        copies = []
        for t, (src, dst) in enumerate(((uf, bu), (itf, bi))):
            for n in range(PAIR):
                at = pl.ds(pl.multiple_of(chosen[PAIR * p + n] * rows, rows), rows)
                to = pl.ds(n * rows, rows)
                copies.append(pltpu.make_async_copy(src.at[at], dst.at[slot, to], bsem.at[slot, t, n]))
        return copies

    @pl.when(pairs > 0)
    def _():
        for copy in fetch(0)[:PAIR]:
            copy.start()

    for copy in loads[2:]:
        copy.start()

    @pl.when(pairs > 0)
    def _():
        for copy in fetch(0)[PAIR:]:
            copy.start()

    def clear(n, carry):
        at = pl.ds(pl.multiple_of(n * 64, 64), 64)
        us_out[at, :] = jnp.zeros((64, width), BF16)
        is_out[at, :] = jnp.zeros((64, width), BF16)
        return carry

    first = columns(lax.axis_index("client"), 0)
    ahead = [pltpu.make_async_copy(src.at[:, first], dst, sem.at[4 + t])
             for t, (src, dst) in enumerate(((uf, cu_out), (itf, ci_out)))]
    lax.fori_loop(0, clients * rows // 64, clear, 0)
    loads[1].wait()

    def rest():
        for copy in loads[2:]:
            copy.wait()
        for copy in ahead:
            copy.start()

    @pl.when(pairs == 0)
    def _():
        rest()

    def pair(p, carry):
        slot = p % 2
        for copy in fetch(p)[:PAIR]:
            copy.wait()
        pre = dot(bu[slot], wu[...])
        sig = 0.5 * jnp.tanh(0.5 * pre) + 0.5
        u = pre * sig
        uvec[...] = u.astype(BF16)
        dsilu[...] = sig + (u - u * sig)
        for copy in fetch(p)[PAIR:]:
            copy.wait()

        @pl.when(p == 0)
        def _():
            rest()

        @pl.when(p + 1 < pairs)
        def _():
            for copy in fetch(p + 1):
                copy.start()

        iv[...] = dot(bi[slot], wi[...]).astype(BF16)
        for n in range(PAIR):
            client = chosen[PAIR * p + n]
            at = slice(n * rows, (n + 1) * rows)
            u = uvec[at, :]
            v = iv[at, :]
            s = dot(u, v, ((1,), (1,))) * temper
            start = client * rows
            same = same_item(ids, start // 128, start % 128, rows)
            gate = 0.5 * jnp.tanh(0.5 * s) + 0.5
            slope = (jnp.where(same, gate - 1.0, gate) * temper).astype(BF16)
            to = pl.ds(pl.multiple_of(start, rows), rows)
            us_out[to, :] = (dot(slope, v) * dsilu[at, :]).astype(BF16)
            is_out[to, :] = dot(slope, u, ((0,), (0,))).astype(BF16)
        return carry

    lax.fori_loop(0, pairs, pair, 0)
    for copy in ahead:
        copy.wait()


def kernel(cfg, uf, itf, ids_hbm, uw, iw, us, its, cu, ci, fin, table,
           ids, fu, fi, wu, wi, iv, uvec, gt, crecv, ya, yb,
           xa1, xal, xar, xb1, xbl, xbr,
           ld, cs, cr, ys, yr, xs, xr, ls, lr, up, down):
    clients, rows, width, split, groups, clusters = cfg
    total, depth = fu.shape
    per = clients // groups
    grp = per * rows
    temper = 1.0 / math.sqrt(width)
    k_me = lax.axis_index("cluster")
    s_me = lax.axis_index("client")
    x = s_me // 4
    y = (s_me // 2) % 2
    c = s_me % 2
    mate = {"client": x * 4 + y * 2 + (1 - c)}
    across = {"client": x * 4 + (1 - y) * 2 + c}
    right = {"client": ((x + 1) % NX) * 4 + y * 2 + c}
    left = {"client": ((x + NX - 1) % NX) * 4 + y * 2 + c}
    nz = clusters // 2
    h = k_me // nz
    z = k_me % nz
    twin = {"cluster": (1 - h) * nz + z}
    above = {"cluster": h * nz + (z + 1) % nz}
    below = {"cluster": h * nz + (z + nz - 1) % nz}
    has_above = z < nz - 1
    has_below = z > 0

    barrier = pltpu.get_barrier_semaphore()
    for peer in (mate, across, right, left, twin):
        pl.semaphore_signal(barrier, inc=1, device_id=peer, device_id_type=MESH)
    for there, peer in ((has_above, above), (has_below, below)):
        @pl.when(there)
        def _(peer=peer):
            pl.semaphore_signal(barrier, inc=1, device_id=peer, device_id_type=MESH)

    def feats(step, t):
        src, dst = ((uf, fu), (itf, fi))[t]
        at = columns(s_me, step)
        return pltpu.make_async_copy(src.at[:, at], dst.at[:, at], ld.at[step, t])

    rest_loads = [pltpu.make_async_copy(src, dst, ld.at[2 * NX, n]) for n, (src, dst) in enumerate(
        ((uw.at[0], wu), (iw.at[0], wi), (ids_hbm, ids)))]
    for step in (1, 2):
        for t in (0, 1):
            feats(step, t).start()

    A = pl.ds(0, split)
    B = pl.ds(split, 128 - split)

    def step_of(dx, dy):
        return STEPS.index((dx, dy))

    def own(dx, dy, t, part):
        return gt.at[step_of(dx, dy), t, c, part]

    def send(src, dst, ssem, rsem, peer):
        return pltpu.make_async_remote_copy(src_ref=src, dst_ref=dst, send_sem=ssem, recv_sem=rsem,
                                            device_id=peer, device_id_type=MESH)

    def pass_on(sem, has_source, has_target, target):
        @pl.when(has_source)
        def _():
            pl.semaphore_wait(sem, 1)

        @pl.when(has_target)
        def _():
            pl.semaphore_signal(sem, inc=1, device_id=target, device_id_type=MESH)

    def tell(n):
        @pl.when((z + 1) // 2 == n)
        def _():
            pass_on(up, has_below, has_above, above)

        @pl.when((nz - z) // 2 == n)
        def _():
            pass_on(down, has_above, has_below, below)

    def loss_copy(n):
        mine = table.at[h, z]
        return send(mine, mine, ls.at[n], lr.at[n], {"cluster": (k_me + n) % clusters})

    def core_copy(step, t):
        return send(gt.at[step, t, 1 - c], crecv.at[step, t], cs.at[step, t], cr.at[step, t], mate)

    def ya_copy(dx, t):
        return send(own(dx, 1, t, A), ya.at[dx, t], ys.at[dx, t], yr.at[dx, t], across)

    def yb_copy(t):
        return send(own(0, 1, t, B), yb.at[t], ys.at[4, t], yr.at[4, t], across)

    def x_part(which):
        return (0, A, xa1, xal, xar) if which == 2 else (which, B, xb1.at[which], xbl.at[which], xbr.at[which])

    def far_copy(which, t):
        dy, part, first, _, _ = x_part(which)
        return send(own(2, dy, t, part), first.at[t], xs.at[which, 0, t], xr.at[which, 0, t], (right, left)[t])

    def near_copy(which, t, rightward):
        dy, part, _, from_left, from_right = x_part(which)
        if rightward:
            return send(own(1, dy, t, part), from_left.at[t], xs.at[which, 1, t], xr.at[which, 1, t], right)
        return send(own(3, dy, t, part), from_right.at[t], xs.at[which, 2, t], xr.at[which, 2, t], left)

    def add(dst, src):
        dst[...] += src[...]

    def far_arrived(which, t):
        dy, part, first, _, _ = x_part(which)
        far_copy(which, t).wait_recv()
        add(own((1, 3)[t], dy, t, part), first.at[t])
        near_copy(which, t, t == 0).start()

    def near_arrived(which):
        dy, part, _, from_left, from_right = x_part(which)
        for t in (0, 1):
            near_copy(which, t, True).wait_recv()
            near_copy(which, t, False).wait_recv()
            mine = own(0, dy, t, part)
            mine[...] += from_left[t] + from_right[t]

    def ya_arrived(dx):
        for t in (0, 1):
            ya_copy(dx, t).wait_recv()
            add(own(dx, 0, t, A), ya.at[dx, t])

    def ready(step, t):
        dx, dy = STEPS[step]
        core_copy(step, t).wait_recv()
        mine = gt.at[step, t, c]
        mine[...] += crecv[step, t]
        if dx == 2:
            far_copy(dy, t).start()
        if dy == 1:
            ya_copy(dx, t).start()
        if dx == 1 and t == 1:
            near_copy(dy, 1, True).start()
        if dx == 3 and t == 0:
            near_copy(dy, 0, False).start()

    def block(step, lhs):
        for t, (slope, feat) in enumerate(((us, lhs[0]), (its, lhs[1]))):
            r = dot(feat(), slope[...], ((0,), (0,)))
            gt[step, t, 0] = r[:128]
            gt[step, t, 1] = r[128:]
            if isinstance(step, int) and step == 0 and t == 0:
                ends = (z + nz - 2) // (nz - 1) + (2 * nz - 3 - z) // (nz - 1)
                pl.semaphore_wait(barrier, 5 + ends)
                tell(0)
            core_copy(step, t).start()
            for n in range(2 * NX - 2):
                if not isinstance(step, int):
                    @pl.when(step == n + 1)
                    def _(n=n, t=t):
                        ready(n, t)

    def loaded(step):
        def of(t, buf):
            feats(step, t).wait()
            return buf[:, columns(s_me, step)]
        return functools.partial(of, 0, fu), functools.partial(of, 1, fi)

    def blocks(step, carry):
        @pl.when(step + 2 < 2 * NX)
        def _():
            for t in (0, 1):
                feats(step + 2, t).start()

        @pl.when(step == 2 * NX - 3)
        def _():
            for copy in rest_loads:
                copy.start()
            for t in (0, 1):
                feats(0, t).start()

        block(step, loaded(step))
        for which in (1, 0):
            @pl.when(step == 2 * NX - 2 - which)
            def _(which=which):
                far_arrived(which, 0)
                far_arrived(which, 1)

        return carry

    block(0, (lambda: cu[...], lambda: ci[...]))
    lax.fori_loop(1, 2 * NX - 1, blocks, 0)
    ready(2 * NX - 2, 0)
    ready(2 * NX - 2, 1)
    for copy in rest_loads:
        copy.wait()
    for t in (0, 1):
        feats(0, t).wait()
        feats(2 * NX - 1, t).wait()

    lane = lax.broadcasted_iota(jnp.int32, (1, 128), 1)

    def losses_of(g, losses):
        at = pl.ds(pl.multiple_of(g * grp, grp), grp)
        pre = dot(fu[at, :], wu[...])
        uvec[...] = (pre * (0.5 * jnp.tanh(0.5 * pre) + 0.5)).astype(BF16)
        iv[...] = dot(fi[at, :], wi[...]).astype(BF16)
        for n in range(per):
            rows_n = slice(n * rows, (n + 1) * rows)
            s = dot(uvec[rows_n, :], iv[rows_n, :], ((1,), (1,))) * temper
            first, off = divmod(n * rows, 128)
            same = same_item(ids, g * (grp // 128) + first, off, rows)
            pair = jnp.maximum(s, 0.0) + jnp.log(1.0 + jnp.exp(-jnp.abs(s))) - jnp.where(same, s, 0.0)
            mean = jnp.sum(pair, axis=(0, 1), keepdims=True) * (1.0 / (rows * rows))
            losses = jnp.where(lane == g * per + n, mean, losses)

        for m in range(groups):
            @pl.when(g == m)
            def _(m=m):
                tell(m + 1)

        @pl.when(g == 0)
        def _():
            ya_arrived(2)
            far_copy(2, 0).start()
            far_copy(2, 1).start()

        @pl.when(g == 1)
        def _():
            ya_arrived(1)
            near_copy(2, 1, True).start()

        return losses

    losses = lax.fori_loop(0, groups, losses_of, jnp.zeros((1, 128), F32))
    table[h, z] = losses
    for n in range(1, clusters):
        loss_copy(n).start()
    near_arrived(1)
    yb_copy(0).start()
    yb_copy(1).start()
    ya_arrived(3)
    near_copy(2, 0, False).start()
    block(2 * NX - 1, (lambda: fu[:, columns(s_me, 2 * NX - 1)], lambda: fi[:, columns(s_me, 2 * NX - 1)]))
    ready(2 * NX - 1, 0)
    ready(2 * NX - 1, 1)
    far_arrived(2, 0)
    far_arrived(2, 1)
    near_arrived(0)
    ya_arrived(0)
    for t in (0, 1):
        yb_copy(t).wait_recv()
        fin[t, split:, :] = gt[step_of(0, 0), t, c, split:, :] + yb[t]
    for t in (0, 1):
        near_copy(2, t, True).wait_recv()
        near_copy(2, t, False).wait_recv()
        fin[t, :split, :] = gt[step_of(0, 0), t, c, :split, :] + xal[t] + xar[t]

    for n in range(1, clusters):
        loss_copy(n).wait()
    for step in range(2 * NX):
        for t in (0, 1):
            core_copy(step, t).wait_send()
    for t in (0, 1):
        for dx in range(NX):
            ya_copy(dx, t).wait_send()
        yb_copy(t).wait_send()
        for which in range(3):
            far_copy(which, t).wait_send()
            near_copy(which, t, True).wait_send()
            near_copy(which, t, False).wait_send()


def finish(fin, table, loss_out, ug_out, ig_out):
    clients, clusters = loss_out.shape
    ug_out[0] = fin[0]
    ig_out[0] = fin[1]
    loss_out[...] = table[...].reshape(clusters, 128).T[:clients, :]


def body(user_feats, item_feats, item_ids, picks, user_weight, item_weight):
    clients = picks.shape[0]
    total, depth = user_feats.shape
    rows = total // clients
    width = user_weight.shape[2]
    clusters = lax.axis_size("cluster")
    groups = 4
    grp = total // groups
    split = 56
    rest = 128 - split
    vmem = pltpu.VMEM
    dma = pltpu.SemaphoreType.DMA
    hbm_spec = pl.BlockSpec(memory_space=pltpu.HBM)
    vmem_spec = pl.BlockSpec(memory_space=pltpu.VMEM)
    uf, itf, ids, picks, uw, iw = [pltpu.with_memory_space_constraint(a, pltpu.HBM) for a in (
        user_feats, item_feats, item_ids.reshape(total // 128, 128), picks, user_weight, item_weight)]
    us, its, cu, ci = pl.pallas_call(
        functools.partial(picked, (clients, rows, width)),
        out_shape=tuple(jax.ShapeDtypeStruct((total, n), BF16) for n in (width, width, 256, 256)),
        in_specs=[hbm_spec] * 6,
        out_specs=(vmem_spec,) * 4,
        scratch_shapes=[
            vmem((total // 128, 128), jnp.int32), pltpu.SMEM((clients,), jnp.int32), pltpu.SMEM((clients,), jnp.int32),
            vmem((depth, width), BF16), vmem((depth, width), BF16),
            vmem((2, PAIR * rows, depth), BF16), vmem((2, PAIR * rows, depth), BF16),
            vmem((PAIR * rows, width), F32), vmem((PAIR * rows, width), BF16), vmem((PAIR * rows, width), BF16),
            dma((6,)), dma((2, 2, PAIR)),
        ],
        compiler_params=pltpu.CompilerParams(vmem_limit_bytes=PICKED_BYTES),
        name="picked",
    )(uf, itf, ids, picks, uw, iw)
    fin, table = pl.pallas_call(
        functools.partial(kernel, (clients, rows, width, split, groups, clusters)),
        out_shape=(jax.ShapeDtypeStruct((2, 128, width), F32), jax.ShapeDtypeStruct((2, clusters // 2, 1, 128), F32)),
        in_specs=[hbm_spec] * 5 + [vmem_spec] * 4,
        out_specs=(vmem_spec, vmem_spec),
        scratch_shapes=[
            vmem((total // 128, 128), jnp.int32),
            vmem((total, depth), BF16), vmem((total, depth), BF16),
            vmem((depth, width), BF16), vmem((depth, width), BF16),
            vmem((grp, width), BF16), vmem((grp, width), BF16),
            vmem((8, 2, 2, 128, width), F32), vmem((8, 2, 128, width), F32),
            vmem((4, 2, split, width), F32), vmem((2, rest, width), F32),
            vmem((2, split, width), F32), vmem((2, split, width), F32), vmem((2, split, width), F32),
            vmem((2, 2, rest, width), F32), vmem((2, 2, rest, width), F32), vmem((2, 2, rest, width), F32),
            dma((2 * NX + 1, 3)), dma((8, 2)), dma((8, 2)), dma((5, 2)), dma((5, 2)),
            dma((3, 3, 2)), dma((3, 3, 2)), dma((clusters,)), dma((clusters,)),
            pltpu.SemaphoreType.REGULAR, pltpu.SemaphoreType.REGULAR,
        ],
        compiler_params=pltpu.CompilerParams(
            collective_id=0, has_side_effects=True, vmem_limit_bytes=ROUND_BYTES),
        name="round",
    )(uf, itf, ids, uw, iw, us, its, cu, ci)
    return pl.pallas_call(
        finish,
        out_shape=(
            jax.ShapeDtypeStruct((clients, clusters), F32),
            jax.ShapeDtypeStruct((1, depth // 16, width), F32),
            jax.ShapeDtypeStruct((1, depth // 16, width), F32),
        ),
        in_specs=[vmem_spec, vmem_spec],
        out_specs=(vmem_spec, vmem_spec, vmem_spec),
        compiler_params=pltpu.CompilerParams(vmem_limit_bytes=FINISH_BYTES),
        name="finish",
    )(fin, table)


def solution(mesh):
    in_specs = (P("client", None), P("client", None), P("client"), P("client"),
                P("cluster", None, None), P("cluster", None, None))
    out_specs = (P("client", None), P("cluster", "client", None), P("cluster", "client", None))
    return jax.shard_map(body, mesh=mesh, in_specs=in_specs, out_specs=out_specs, check_vma=False)
```

```python
import functools
import math

import jax
import jax.numpy as jnp
from jax import lax
from jax.experimental import pallas as pl
from jax.experimental.pallas import tpu as pltpu
from jax.sharding import PartitionSpec as P

MESH = pl.DeviceIdType.MESH
NX = 4
STEPS = ((2, 1), (2, 0), (1, 1), (3, 1), (1, 0), (3, 0), (0, 1), (0, 0))
PAIR = 2
PICKED_BYTES = 24 * 1024 * 1024
ROUND_BYTES = 46 * 1024 * 1024
FINISH_BYTES = 8 * 1024 * 1024
F32, BF16 = jnp.float32, jnp.bfloat16


def dot(a, b, dims=((1,), (0,))):
    return lax.dot_general(a, b, (dims, ((), ())), preferred_element_type=F32)


def same_item(ids, first, off, rows):
    shape = (rows, 128)
    last = ids.shape[0] - 1
    back = (128 - off) % 128
    got = pltpu.roll(jnp.broadcast_to(ids[pl.ds(first, 1), :], shape), back, 1)
    more = pltpu.roll(jnp.broadcast_to(ids[pl.ds(jnp.minimum(first + 1, last), 1), :], shape), back, 1)
    got = jnp.where(lax.broadcasted_iota(jnp.int32, shape, 1) < 128 - off, got, more)[:, :rows]
    return got == got.T


def columns(s_me, step):
    q = (step + 2) // 4
    middle = q * (2 - q)
    dx = (1 - q) * (2 - q) + middle * (1 + 2 * (step % 2))
    dy = middle * (2 - step // 2) + (1 - middle) * (1 - step % 2)
    chip = ((s_me // 4 + dx) % NX) * 2 + ((s_me // 2) % 2 + dy) % 2
    return pl.ds(pl.multiple_of(chip * 256, 256), 256)


def picked(cfg, uf, itf, ids_hbm, picks_hbm, uw, iw, us_out, is_out, cu_out, ci_out,
           ids, picks, chosen, wu, wi, bu, bi, dsilu, uvec, iv, sem, bsem):
    clients, rows, width = cfg
    temper = 1.0 / math.sqrt(width)
    k_me = lax.axis_index("cluster")
    loads = [pltpu.make_async_copy(src, dst, sem.at[n]) for n, (src, dst) in enumerate(
        ((picks_hbm, picks), (uw.at[0], wu), (iw.at[0], wi), (ids_hbm, ids)))]
    for copy in loads:
        copy.start()
    loads[0].wait()

    def scan(client, count):
        chosen[count] = client
        return count + jnp.where(picks[client] == k_me, 1, 0)

    count = lax.fori_loop(0, clients, scan, 0)

    @pl.when(count % PAIR == 1)
    def _():
        chosen[count] = chosen[count - 1]

    pairs = (count + 1) // PAIR

    def fetch(p):
        slot = p % 2
        copies = []
        for n in range(PAIR):
            at = pl.ds(pl.multiple_of(chosen[PAIR * p + n] * rows, rows), rows)
            to = pl.ds(n * rows, rows)
            copies.append(pltpu.make_async_copy(uf.at[at], bu.at[slot, to], bsem.at[slot, 0, n]))
            copies.append(pltpu.make_async_copy(itf.at[at], bi.at[slot, to], bsem.at[slot, 1, n]))
        return copies

    @pl.when(pairs > 0)
    def _():
        for copy in fetch(0):
            copy.start()

    def clear(n, carry):
        at = pl.ds(pl.multiple_of(n * 64, 64), 64)
        us_out[at, :] = jnp.zeros((64, width), BF16)
        is_out[at, :] = jnp.zeros((64, width), BF16)
        return carry

    first = columns(lax.axis_index("client"), 0)
    ahead = [pltpu.make_async_copy(src.at[:, first], dst, sem.at[4 + t])
             for t, (src, dst) in enumerate(((uf, cu_out), (itf, ci_out)))]
    for copy in ahead:
        copy.start()
    lax.fori_loop(0, clients * rows // 64, clear, 0)
    for copy in loads[1:]:
        copy.wait()

    def pair(p, carry):
        slot = p % 2

        @pl.when(p + 1 < pairs)
        def _():
            for copy in fetch(p + 1):
                copy.start()

        for copy in fetch(p):
            copy.wait()
        pre = dot(bu[slot], wu[...])
        sig = 0.5 * jnp.tanh(0.5 * pre) + 0.5
        u = pre * sig
        uvec[...] = u.astype(BF16)
        dsilu[...] = sig + (u - u * sig)
        iv[...] = dot(bi[slot], wi[...]).astype(BF16)
        for n in range(PAIR):
            client = chosen[PAIR * p + n]
            at = slice(n * rows, (n + 1) * rows)
            u = uvec[at, :]
            v = iv[at, :]
            s = dot(u, v, ((1,), (1,))) * temper
            start = client * rows
            same = same_item(ids, start // 128, start % 128, rows)
            gate = 0.5 * jnp.tanh(0.5 * s) + 0.5
            slope = (jnp.where(same, gate - 1.0, gate) * temper).astype(BF16)
            to = pl.ds(pl.multiple_of(start, rows), rows)
            us_out[to, :] = (dot(slope, v) * dsilu[at, :]).astype(BF16)
            is_out[to, :] = dot(slope, u, ((0,), (0,))).astype(BF16)
        return carry

    lax.fori_loop(0, pairs, pair, 0)
    for copy in ahead:
        copy.wait()


def kernel(cfg, uf, itf, ids_hbm, uw, iw, us, its, cu, ci, fin, table,
           ids, fu, fi, wu, wi, iv, uvec, gt, crecv, ya, yb,
           xa1, xal, xar, xb1, xbl, xbr,
           ld, cs, cr, ys, yr, xs, xr, ls, lr, up, down):
    clients, rows, width, split, groups, clusters = cfg
    total, depth = fu.shape
    per = clients // groups
    grp = per * rows
    temper = 1.0 / math.sqrt(width)
    k_me = lax.axis_index("cluster")
    s_me = lax.axis_index("client")
    x = s_me // 4
    y = (s_me // 2) % 2
    c = s_me % 2
    mate = {"client": x * 4 + y * 2 + (1 - c)}
    across = {"client": x * 4 + (1 - y) * 2 + c}
    right = {"client": ((x + 1) % NX) * 4 + y * 2 + c}
    left = {"client": ((x + NX - 1) % NX) * 4 + y * 2 + c}
    nz = clusters // 2
    h = k_me // nz
    z = k_me % nz
    twin = {"cluster": (1 - h) * nz + z}
    above = {"cluster": h * nz + (z + 1) % nz}
    below = {"cluster": h * nz + (z + nz - 1) % nz}
    has_above = z < nz - 1
    has_below = z > 0

    barrier = pltpu.get_barrier_semaphore()
    for peer in (mate, across, right, left, twin):
        pl.semaphore_signal(barrier, inc=1, device_id=peer, device_id_type=MESH)
    for there, peer in ((has_above, above), (has_below, below)):
        @pl.when(there)
        def _(peer=peer):
            pl.semaphore_signal(barrier, inc=1, device_id=peer, device_id_type=MESH)

    def feats(step, t):
        src, dst = ((uf, fu), (itf, fi))[t]
        at = columns(s_me, step)
        return pltpu.make_async_copy(src.at[:, at], dst.at[:, at], ld.at[step, t])

    rest_loads = [pltpu.make_async_copy(src, dst, ld.at[2 * NX, n]) for n, (src, dst) in enumerate(
        ((uw.at[0], wu), (iw.at[0], wi), (ids_hbm, ids)))]
    for step in (1, 2):
        for t in (0, 1):
            feats(step, t).start()

    A = pl.ds(0, split)
    B = pl.ds(split, 128 - split)

    def step_of(dx, dy):
        return STEPS.index((dx, dy))

    def own(dx, dy, t, part):
        return gt.at[step_of(dx, dy), t, c, part]

    def send(src, dst, ssem, rsem, peer):
        return pltpu.make_async_remote_copy(src_ref=src, dst_ref=dst, send_sem=ssem, recv_sem=rsem,
                                            device_id=peer, device_id_type=MESH)

    def pass_on(sem, has_source, has_target, target):
        @pl.when(has_source)
        def _():
            pl.semaphore_wait(sem, 1)

        @pl.when(has_target)
        def _():
            pl.semaphore_signal(sem, inc=1, device_id=target, device_id_type=MESH)

    def tell(n):
        @pl.when((z + 1) // 2 == n)
        def _():
            pass_on(up, has_below, has_above, above)

        @pl.when((nz - z) // 2 == n)
        def _():
            pass_on(down, has_above, has_below, below)

    def loss_copy(n):
        mine = table.at[h, z]
        return send(mine, mine, ls.at[n], lr.at[n], {"cluster": (k_me + n) % clusters})

    def core_copy(step, t):
        return send(gt.at[step, t, 1 - c], crecv.at[step, t], cs.at[step, t], cr.at[step, t], mate)

    def ya_copy(dx, t):
        return send(own(dx, 1, t, A), ya.at[dx, t], ys.at[dx, t], yr.at[dx, t], across)

    def yb_copy(t):
        return send(own(0, 1, t, B), yb.at[t], ys.at[4, t], yr.at[4, t], across)

    def x_part(which):
        return (0, A, xa1, xal, xar) if which == 2 else (which, B, xb1.at[which], xbl.at[which], xbr.at[which])

    def far_copy(which, t):
        dy, part, first, _, _ = x_part(which)
        return send(own(2, dy, t, part), first.at[t], xs.at[which, 0, t], xr.at[which, 0, t], (right, left)[t])

    def near_copy(which, t, rightward):
        dy, part, _, from_left, from_right = x_part(which)
        if rightward:
            return send(own(1, dy, t, part), from_left.at[t], xs.at[which, 1, t], xr.at[which, 1, t], right)
        return send(own(3, dy, t, part), from_right.at[t], xs.at[which, 2, t], xr.at[which, 2, t], left)

    def add(dst, src):
        dst[...] += src[...]

    def far_arrived(which, t):
        dy, part, first, _, _ = x_part(which)
        far_copy(which, t).wait_recv()
        add(own((1, 3)[t], dy, t, part), first.at[t])
        near_copy(which, t, t == 0).start()

    def near_arrived(which):
        dy, part, _, from_left, from_right = x_part(which)
        for t in (0, 1):
            near_copy(which, t, True).wait_recv()
            near_copy(which, t, False).wait_recv()
            mine = own(0, dy, t, part)
            mine[...] += from_left[t] + from_right[t]

    def ya_arrived(dx):
        for t in (0, 1):
            ya_copy(dx, t).wait_recv()
            add(own(dx, 0, t, A), ya.at[dx, t])

    def ready(step, t):
        dx, dy = STEPS[step]
        core_copy(step, t).wait_recv()
        mine = gt.at[step, t, c]
        mine[...] += crecv[step, t]
        if dx == 2:
            far_copy(dy, t).start()
        if dy == 1:
            ya_copy(dx, t).start()
        if dx == 1 and t == 1:
            near_copy(dy, 1, True).start()
        if dx == 3 and t == 0:
            near_copy(dy, 0, False).start()

    def block(step, lhs):
        for t, (slope, feat) in enumerate(((us, lhs[0]), (its, lhs[1]))):
            r = dot(feat(), slope[...], ((0,), (0,)))
            gt[step, t, 0] = r[:128]
            gt[step, t, 1] = r[128:]
            if isinstance(step, int) and step == 0 and t == 0:
                ends = (z + nz - 2) // (nz - 1) + (2 * nz - 3 - z) // (nz - 1)
                pl.semaphore_wait(barrier, 5 + ends)
                tell(0)
            core_copy(step, t).start()
            for n in range(2 * NX - 2):
                if not isinstance(step, int):
                    @pl.when(step == n + 1)
                    def _(n=n, t=t):
                        ready(n, t)

    def loaded(step):
        def of(t, buf):
            feats(step, t).wait()
            return buf[:, columns(s_me, step)]
        return functools.partial(of, 0, fu), functools.partial(of, 1, fi)

    def blocks(step, carry):
        @pl.when(step + 2 < 2 * NX)
        def _():
            for t in (0, 1):
                feats(step + 2, t).start()

        @pl.when(step == 2 * NX - 3)
        def _():
            for copy in rest_loads:
                copy.start()
            for t in (0, 1):
                feats(0, t).start()

        block(step, loaded(step))
        for which in (1, 0):
            @pl.when(step == 2 * NX - 2 - which)
            def _(which=which):
                far_arrived(which, 0)
                far_arrived(which, 1)

        return carry

    block(0, (lambda: cu[...], lambda: ci[...]))
    lax.fori_loop(1, 2 * NX - 1, blocks, 0)
    ready(2 * NX - 2, 0)
    ready(2 * NX - 2, 1)
    for copy in rest_loads:
        copy.wait()
    for t in (0, 1):
        feats(0, t).wait()
        feats(2 * NX - 1, t).wait()

    lane = lax.broadcasted_iota(jnp.int32, (1, 128), 1)

    def losses_of(g, losses):
        at = pl.ds(pl.multiple_of(g * grp, grp), grp)
        pre = dot(fu[at, :], wu[...])
        uvec[...] = (pre * (0.5 * jnp.tanh(0.5 * pre) + 0.5)).astype(BF16)
        iv[...] = dot(fi[at, :], wi[...]).astype(BF16)
        for n in range(per):
            rows_n = slice(n * rows, (n + 1) * rows)
            s = dot(uvec[rows_n, :], iv[rows_n, :], ((1,), (1,))) * temper
            first, off = divmod(n * rows, 128)
            same = same_item(ids, g * (grp // 128) + first, off, rows)
            pair = jnp.maximum(s, 0.0) + jnp.log(1.0 + jnp.exp(-jnp.abs(s))) - jnp.where(same, s, 0.0)
            mean = jnp.sum(pair, axis=(0, 1), keepdims=True) * (1.0 / (rows * rows))
            losses = jnp.where(lane == g * per + n, mean, losses)

        for m in range(groups):
            @pl.when(g == m)
            def _(m=m):
                tell(m + 1)

        @pl.when(g == 0)
        def _():
            ya_arrived(2)
            far_copy(2, 0).start()
            far_copy(2, 1).start()

        @pl.when(g == 1)
        def _():
            ya_arrived(1)
            near_copy(2, 1, True).start()

        return losses

    losses = lax.fori_loop(0, groups, losses_of, jnp.zeros((1, 128), F32))
    table[h, z] = losses
    for n in range(1, clusters):
        loss_copy(n).start()
    near_arrived(1)
    yb_copy(0).start()
    yb_copy(1).start()
    ya_arrived(3)
    near_copy(2, 0, False).start()
    block(2 * NX - 1, (lambda: fu[:, columns(s_me, 2 * NX - 1)], lambda: fi[:, columns(s_me, 2 * NX - 1)]))
    ready(2 * NX - 1, 0)
    ready(2 * NX - 1, 1)
    far_arrived(2, 0)
    far_arrived(2, 1)
    near_arrived(0)
    ya_arrived(0)
    for t in (0, 1):
        yb_copy(t).wait_recv()
        fin[t, split:, :] = gt[step_of(0, 0), t, c, split:, :] + yb[t]
    for t in (0, 1):
        near_copy(2, t, True).wait_recv()
        near_copy(2, t, False).wait_recv()
        fin[t, :split, :] = gt[step_of(0, 0), t, c, :split, :] + xal[t] + xar[t]

    for n in range(1, clusters):
        loss_copy(n).wait()
    for step in range(2 * NX):
        for t in (0, 1):
            core_copy(step, t).wait_send()
    for t in (0, 1):
        for dx in range(NX):
            ya_copy(dx, t).wait_send()
        yb_copy(t).wait_send()
        for which in range(3):
            far_copy(which, t).wait_send()
            near_copy(which, t, True).wait_send()
            near_copy(which, t, False).wait_send()


def finish(fin, table, loss_out, ug_out, ig_out):
    clients, clusters = loss_out.shape
    ug_out[0] = fin[0]
    ig_out[0] = fin[1]
    loss_out[...] = table[...].reshape(clusters, 128).T[:clients, :]


def body(user_feats, item_feats, item_ids, picks, user_weight, item_weight):
    clients = picks.shape[0]
    total, depth = user_feats.shape
    rows = total // clients
    width = user_weight.shape[2]
    clusters = lax.axis_size("cluster")
    groups = 4
    grp = total // groups
    split = 56
    rest = 128 - split
    vmem = pltpu.VMEM
    dma = pltpu.SemaphoreType.DMA
    hbm_spec = pl.BlockSpec(memory_space=pltpu.HBM)
    vmem_spec = pl.BlockSpec(memory_space=pltpu.VMEM)
    uf, itf, ids, picks, uw, iw = [pltpu.with_memory_space_constraint(a, pltpu.HBM) for a in (
        user_feats, item_feats, item_ids.reshape(total // 128, 128), picks, user_weight, item_weight)]
    us, its, cu, ci = pl.pallas_call(
        functools.partial(picked, (clients, rows, width)),
        out_shape=tuple(jax.ShapeDtypeStruct((total, n), BF16) for n in (width, width, 256, 256)),
        in_specs=[hbm_spec] * 6,
        out_specs=(vmem_spec,) * 4,
        scratch_shapes=[
            vmem((total // 128, 128), jnp.int32), pltpu.SMEM((clients,), jnp.int32), pltpu.SMEM((clients,), jnp.int32),
            vmem((depth, width), BF16), vmem((depth, width), BF16),
            vmem((2, PAIR * rows, depth), BF16), vmem((2, PAIR * rows, depth), BF16),
            vmem((PAIR * rows, width), F32), vmem((PAIR * rows, width), BF16), vmem((PAIR * rows, width), BF16),
            dma((6,)), dma((2, 2, PAIR)),
        ],
        compiler_params=pltpu.CompilerParams(vmem_limit_bytes=PICKED_BYTES),
        name="picked",
    )(uf, itf, ids, picks, uw, iw)
    fin, table = pl.pallas_call(
        functools.partial(kernel, (clients, rows, width, split, groups, clusters)),
        out_shape=(jax.ShapeDtypeStruct((2, 128, width), F32), jax.ShapeDtypeStruct((2, clusters // 2, 1, 128), F32)),
        in_specs=[hbm_spec] * 5 + [vmem_spec] * 4,
        out_specs=(vmem_spec, vmem_spec),
        scratch_shapes=[
            vmem((total // 128, 128), jnp.int32),
            vmem((total, depth), BF16), vmem((total, depth), BF16),
            vmem((depth, width), BF16), vmem((depth, width), BF16),
            vmem((grp, width), BF16), vmem((grp, width), BF16),
            vmem((8, 2, 2, 128, width), F32), vmem((8, 2, 128, width), F32),
            vmem((4, 2, split, width), F32), vmem((2, rest, width), F32),
            vmem((2, split, width), F32), vmem((2, split, width), F32), vmem((2, split, width), F32),
            vmem((2, 2, rest, width), F32), vmem((2, 2, rest, width), F32), vmem((2, 2, rest, width), F32),
            dma((2 * NX + 1, 3)), dma((8, 2)), dma((8, 2)), dma((5, 2)), dma((5, 2)),
            dma((3, 3, 2)), dma((3, 3, 2)), dma((clusters,)), dma((clusters,)),
            pltpu.SemaphoreType.REGULAR, pltpu.SemaphoreType.REGULAR,
        ],
        compiler_params=pltpu.CompilerParams(
            collective_id=0, has_side_effects=True, vmem_limit_bytes=ROUND_BYTES),
        name="round",
    )(uf, itf, ids, uw, iw, us, its, cu, ci)
    return pl.pallas_call(
        finish,
        out_shape=(
            jax.ShapeDtypeStruct((clients, clusters), F32),
            jax.ShapeDtypeStruct((1, depth // 16, width), F32),
            jax.ShapeDtypeStruct((1, depth // 16, width), F32),
        ),
        in_specs=[vmem_spec, vmem_spec],
        out_specs=(vmem_spec, vmem_spec, vmem_spec),
        compiler_params=pltpu.CompilerParams(vmem_limit_bytes=FINISH_BYTES),
        name="finish",
    )(fin, table)


def solution(mesh):
    in_specs = (P("client", None), P("client", None), P("client"), P("client"),
                P("cluster", None, None), P("cluster", None, None))
    out_specs = (P("client", None), P("cluster", "client", None), P("cluster", "client", None))
    return jax.shard_map(body, mesh=mesh, in_specs=in_specs, out_specs=out_specs, check_vma=False)
```
